1024 devices in a mesh: seq: 128 (over z, y), head: 8 (over x, core).
Axes of the slice: x: 4, y: 8, z: 16, core: 2. Of those that a mesh axis runs over, the one named last changes fastest.
Arguments:
- query_rows: bfloat16 [32, 32768, 128], P('head', 'seq'), may hold values from -6 to 6
- key_rows: bfloat16 [32, 32768, 128], P('head', 'seq'), may hold values from -0.5 to 0.5
- value_rows: bfloat16 [32, 32768, 128], P('head', 'seq'), may hold values from -40 to 40
- log_gate: float32 [32, 32768], P('head', 'seq'), may hold values from -1 to 0
- episode: int32 [32768], P('seq'), may hold values from 0 to 31, never falling along the last dimension, each value on 1 to 4096 neighbouring positions
- grad_out: bfloat16 [32, 32768, 128], P('head', 'seq'), may hold values from -6 to 6
Outputs:
- normed: bfloat16 [32, 32768, 128], P('head', 'seq')
- grad_query: bfloat16 [32, 32768, 128], P('head', 'seq')
- grad_key: bfloat16 [32, 32768, 128], P('head', 'seq')
- grad_value: bfloat16 [32, 32768, 128], P('head', 'seq')
The draws below stay inside these ranges and needn't reach their ends.
Inputs may be any that keep to these rules, and one draw needn't show every extreme that they name: Episode ids never fall along the tokens; every episode spans 1 to 4096 tokens and one spans exactly 4096.
All inputs are finite; a program needn't handle non-finite values.
Results may differ from the reference program's by a relative error of at most 0.0062.
Values sent between devices are 32-bit elements; how exact they have to be, the bound alone decides.
No kernel may reach another device: no remote copies, remote signals or barrier semaphores. Data moves between devices by JAX's collectives and lax.ppermute only.
A program may use at most 32 MiB of HBM per device.

```python
import math
import jax
import jax.numpy as jnp
import numpy as np
from jax import lax

HEAD_DIM = 128
HEADS = 32
STRETCH = 256
TOK_DEV = 256
TOKENS = 32768
EP_MOST = 4096
EPISODES = 32


def draw_value_rows(key, part):
    noise_key, spread_key = jax.random.split(key, 2)
    position = jnp.arange(HEADS, dtype=jnp.float32)[:, None, None] / max(HEADS - 1, 1)
    ramped = jnp.exp(math.log(3.0) * (position - 0.5))
    spread = jnp.exp(math.log(10.0) * (jax.random.uniform(spread_key, (HEADS, 1, HEAD_DIM), jnp.float32) - 0.5))
    result = jax.random.normal(noise_key, (HEADS, TOKENS, HEAD_DIM), jnp.float32) * spread * ramped
    return jnp.clip(result, -40.0, 40.0).astype(jnp.bfloat16)


def draw_log_gate(key, part):
    fast_key, slow_key, quick_key, rough_key, block_key, location_seed, loss_key = jax.random.split(key, 7)
    fraction = 0.5
    fast = jax.random.bernoulli(fast_key, fraction, (HEADS, 1))
    slow_rate = jnp.exp(jax.random.uniform(slow_key, (HEADS, 1), jnp.float32, math.log(0.1), math.log(0.6))) / EP_MOST
    quick_rate = jnp.exp(jax.random.uniform(quick_key, (HEADS, 1), jnp.float32, math.log(1.0 / 50.0), math.log(1.0 / 30.0)))
    forgetting_factors = jnp.where(fast, quick_rate, slow_rate)
    perturbation_broad = jax.random.uniform(rough_key, (HEADS, TOKENS), jnp.float32, 0.5, 2.0)
    partition_sets = jnp.exp(jax.random.uniform(block_key, (HEADS, TOKENS // TOK_DEV), jnp.float32, math.log(0.6), math.log(1.7)))
    partition_sets = jnp.repeat(partition_sets, TOK_DEV, axis=1)
    spots = jax.random.randint(location_seed, (6,), 0, TOKENS)
    restart_markers = jnp.any(jnp.arange(TOKENS)[:, None] == spots[None, :], axis=1)
    objective_outputs = jax.random.uniform(loss_key, (HEADS, TOKENS), jnp.float32, math.log(0.5), math.log(0.8))
    episode_lengths = jnp.where(restart_markers[None, :], objective_outputs, 0.0)
    return (-forgetting_factors * perturbation_broad * partition_sets + episode_lengths).astype(jnp.float32)


def block_scale(rng, extent, shards, low, high):
    level = 1.0
    for dim, blocks in shards:
        steps = jax.random.uniform(jax.random.fold_in(jax.random.fold_in(rng, 6), dim), (blocks,), jnp.float32, low / len(shards), high / len(shards))
        level = level * jnp.repeat(jnp.exp(steps), extent[dim] // blocks).reshape((-1,) + (1,) * (len(extent) - 1 - dim))
    return level


def length_profile(count, total, limit, lean):
    weights = [(1 << 20) // math.isqrt(rank ** lean) + 1 for rank in range(2, count + 1)]
    spare, given = total - limit - (count - 1), [1] * (count - 1)
    while spare > 0:
        candidates = [i for i in range(count - 1) if given[i] < limit]
        whole, left = sum([weights[i] for i in candidates]), spare
        for i in candidates:
            addition = min(limit - given[i], max(1, left * weights[i] // whole), spare)
            given[i] = given[i] + addition
            spare = spare - addition
    return np.array([limit] + given)


def ragged(key, amount, total, bound, lean):
    if amount == 2:
        one = jax.random.randint(key, (), max(1, total - bound), min(bound, total - 1) + 1)
        return jnp.stack([one, total - one])
    sizes = jnp.asarray(length_profile(amount, total, bound, lean), jnp.int32)
    twos = (amount - 1) // 2
    donor, receiver = sizes[1:1 + 2 * twos:2], sizes[2:2 + 2 * twos:2]
    margin = jnp.minimum(donor - 1, bound - receiver)
    passed = jax.random.randint(jax.random.fold_in(key, 1), (twos,), 0, 1 << 20) % (margin + 1)
    sizes = sizes.at[1:1 + 2 * twos:2].set(donor - passed).at[2:2 + 2 * twos:2].set(receiver + passed)
    return sizes[jax.random.permutation(jax.random.fold_in(key, 2), amount)]


def normal_values(key, shape, scale, bound, pieces=(), held_as=jnp.bfloat16):
    array = jax.random.normal(key, shape, jnp.float32) * scale
    if len(pieces) > 0:
        array = block_scale(key, shape, pieces, -0.22, 0.18) * array
    return jnp.clip(array, min=-bound, max=bound).astype(held_as)


def setup_inputs(seed: int = 0) -> dict:
    splits = jax.random.split(jax.random.key(seed), 7)
    return {
        "query_rows": normal_values(splits[0], (HEADS, TOKENS, HEAD_DIM), 1.0, 6.0, ((0, 8), (1, 128))),
        "key_rows": normal_values(splits[1], (HEADS, TOKENS, HEAD_DIM), (HEAD_DIM ** -0.5), 0.5, ((0, 8), (1, 128))),
        "value_rows": draw_value_rows(jax.random.fold_in(splits[6], 71), 0),
        "log_gate": draw_log_gate(jax.random.fold_in(splits[6], 71), 0),
        "episode": jnp.searchsorted(jnp.cumsum(ragged(splits[4], EPISODES, TOKENS, EP_MOST, 2)), jnp.arange(TOKENS), side="right").astype(jnp.int32),
        "grad_out": normal_values(splits[5], (HEADS, TOKENS, HEAD_DIM), 1.0, 6.0, ((0, 8), (1, 128))),
    }


EPSILON = 1e-06

def rounded(values):
    return lax.optimization_barrier(values.astype(jnp.bfloat16)).astype(jnp.float32)

def stretch_terms(gates, episodes):
    running = jnp.cumsum(gates, axis=-1)
    length = episodes.shape[0]
    causal = jnp.arange(length)[:, None] >= jnp.arange(length)[None, :]
    allowed = ((episodes[:, None] == episodes[None, :]) & causal)[None]
    differences = running[:, :, None] - running[:, None, :]
    decays = jnp.where(allowed, jnp.exp(jnp.where(allowed, differences, 0.0)), 0.0)
    return (running, decays)

def reference(query_rows, key_rows, value_rows, log_gate, episode, grad_out):
    head_count, tokens, head_width = query_rows.shape
    stretch_count = tokens // STRETCH

    def split_stretches(values):
        return jnp.moveaxis(values.reshape(head_count, stretch_count, STRETCH, head_width), 1, 0)

    def join_stretches(values):
        return jnp.moveaxis(values, 0, 1).reshape(head_count, tokens, head_width)
    queries = split_stretches(query_rows)
    keyset = split_stretches(key_rows)
    values = split_stretches(value_rows)
    gates = jnp.moveaxis(log_gate.reshape(head_count, stretch_count, STRETCH), 1, 0)
    episodes = episode.reshape(stretch_count, STRETCH)

    def forward_stretch(carried_in, inputs):
        state, previous = carried_in
        stretch_query, stretch_key, stretch_value, stretch_gate, stretch_episode = inputs
        running, decays = stretch_terms(stretch_gate, stretch_episode)
        query_wide = stretch_query.astype(jnp.float32)
        key_wide = stretch_key.astype(jnp.float32)
        value_wide = stretch_value.astype(jnp.float32)
        scores = rounded(jnp.einsum('hcd,hsd->hcs', query_wide, key_wide) * decays)
        within = jnp.einsum('hcs,hse->hce', scores, value_wide)
        state_low = rounded(state)
        carried = jnp.where((stretch_episode == previous)[None, :], jnp.exp(running), 0.0)
        attention = within + jnp.einsum('hcd,hde->hce', query_wide, state_low) * carried[:, :, None]
        last_id = stretch_episode[-1]
        weight = jnp.where((stretch_episode == last_id)[None, :], jnp.exp(running[:, -1:] - running), 0.0)
        keys_decayed = rounded(key_wide * weight[:, :, None])
        local_state = jnp.einsum('hcd,hce->hde', keys_decayed, value_wide)
        kept = jnp.where(previous == last_id, jnp.exp(running[:, -1])[:, None, None] * state, 0.0)
        return ((kept + local_state, last_id), (attention, state_low, previous))
    start = (jnp.zeros((head_count, head_width, head_width), jnp.float32), jnp.int32(-1))
    ignored, (attention_all, state_lows, previous_ids) = lax.scan(forward_stretch, start, (queries, keyset, values, gates, episodes))
    attention = join_stretches(attention_all)
    cotangent = grad_out.astype(jnp.float32)
    features = head_count * head_width
    squared_terms = lax.optimization_barrier(jnp.sum(attention * attention, axis=(0, 2)))
    crossed = lax.optimization_barrier(jnp.sum(cotangent * attention, axis=(0, 2)))
    root_mean = jnp.sqrt(squared_terms / features + EPSILON)
    normed = (attention / root_mean[None, :, None]).astype(jnp.bfloat16)
    grad_attn = ((cotangent - attention * (crossed / (features * root_mean * root_mean))[None, :, None]) / root_mean[None, :, None]).astype(jnp.bfloat16)
    grad_stretches = split_stretches(grad_attn)

    def backward_stretch(carried_in, inputs):
        back, following = carried_in
        stretch_query, stretch_key, stretch_value, stretch_gate, stretch_episode, stretch_grad, state_low, previous = inputs
        running, decays = stretch_terms(stretch_gate, stretch_episode)
        query_wide = stretch_query.astype(jnp.float32)
        key_wide = stretch_key.astype(jnp.float32)
        value_wide = stretch_value.astype(jnp.float32)
        grad_wide = stretch_grad.astype(jnp.float32)
        scores = rounded(jnp.einsum('hcd,hsd->hcs', query_wide, key_wide) * decays)
        score_gradient = rounded(jnp.einsum('hce,hse->hcs', grad_wide, value_wide) * decays)
        carried = jnp.where((stretch_episode == previous)[None, :], jnp.exp(running), 0.0)
        query_grad = jnp.einsum('hcs,hsd->hcd', score_gradient, key_wide) + jnp.einsum('hce,hde->hcd', grad_wide, state_low) * carried[:, :, None]
        back_low = rounded(back)
        trailing = jnp.where((stretch_episode == following)[None, :], jnp.exp(running[:, -1:] - running), 0.0)
        key_grad = jnp.einsum('hcs,hcd->hsd', score_gradient, query_wide) + jnp.einsum('hce,hde->hcd', value_wide, back_low) * trailing[:, :, None]
        value_grad = jnp.einsum('hcs,hce->hse', scores, grad_wide) + jnp.einsum('hcd,hde->hce', key_wide, back_low) * trailing[:, :, None]
        first_id = stretch_episode[0]
        query_weight = jnp.where((stretch_episode == first_id)[None, :], jnp.exp(running), 0.0)
        queries_decayed = rounded(query_wide * query_weight[:, :, None])
        local_back = jnp.einsum('hcd,hce->hde', queries_decayed, grad_wide)
        kept = jnp.where(first_id == following, jnp.exp(running[:, -1])[:, None, None] * back, 0.0)
        outputs = (query_grad.astype(jnp.bfloat16), key_grad.astype(jnp.bfloat16), value_grad.astype(jnp.bfloat16))
        return ((kept + local_back, first_id), outputs)
    ignored_back, (query_grads, key_grads, value_grads) = lax.scan(backward_stretch, start, (queries, keyset, values, gates, episodes, grad_stretches, state_lows, previous_ids), reverse=True)
    return (normed, join_stretches(query_grads), join_stretches(key_grads), join_stretches(value_grads))
```

```python
import functools

import jax
import jax.numpy as jnp
from jax import lax
from jax.experimental import pallas as pl
from jax.experimental.pallas import tpu as pltpu
from jax.sharding import PartitionSpec as P

EPSILON = 1e-06
ROW = 16
META = 8
HIGH = lax.Precision.HIGHEST


def dot(a, b, da, db):
    return lax.dot_general(
        a, b, (((da,), (db,)), ((), ())), preferred_element_type=jnp.float32
    )


def call(body, outs, flops, scratch=()):
    shapes = [jax.ShapeDtypeStruct(s, d) for s, d in outs]

    def run(*args):
        size = sum(a.size * a.dtype.itemsize for a in (*args, *shapes))
        return pl.pallas_call(
            body,
            out_shape=shapes,
            in_specs=[pl.BlockSpec(memory_space=pltpu.VMEM)] * len(args),
            out_specs=[pl.BlockSpec(memory_space=pltpu.VMEM)] * len(shapes),
            scratch_shapes=list(scratch),
            cost_estimate=pl.CostEstimate(flops=flops, bytes_accessed=size, transcendentals=0),
            compiler_params=pltpu.CompilerParams(vmem_limit_bytes=8 << 20),
            name=body.__name__ if hasattr(body, "__name__") else body.func.__name__,
        )(*args)

    return run


def local_states(gate_ref, ep_ref, k_ref, v_ref, pay_ref, rows_ref, cols_ref):
    heads, tokens = gate_ref.shape
    width = k_ref.shape[2]
    per_head = ROW // heads
    depth = width // per_head
    run = gate_ref[...]
    place = lax.broadcasted_iota(jnp.int32, run.shape, 1)
    step = 1
    while step < tokens:
        run = run + jnp.where(place >= step, pltpu.roll(run, step, 1), 0.0)
        step *= 2
    total = run[:, tokens - 1 :]
    ep = ep_ref[...]
    first, last = ep[:, :1], ep[:, tokens - 1 :]
    rows_ref[...] = jnp.zeros(rows_ref.shape, jnp.float32)
    rows_ref[0:heads] = run
    rows_ref[heads : 2 * heads] = jnp.where(ep == first, jnp.exp(run), 0.0)
    rows_ref[2 * heads : 3 * heads] = jnp.where(ep == last, jnp.exp(total - run), 0.0)
    rows_ref[3 * heads : 3 * heads + 1] = ep.astype(jnp.float32)
    cols_ref[...] = rows_ref[...].T
    fact = lax.broadcasted_iota(jnp.int32, (META, width), 0)
    first_f, last_f = first.astype(jnp.float32), last.astype(jnp.float32)
    for h in range(heads):
        leave = cols_ref[:, 2 * heads + h : 2 * heads + h + 1]
        decayed = (k_ref[h].astype(jnp.float32) * leave).astype(jnp.bfloat16)
        state = dot(decayed, v_ref[h], 0, 0)
        facts = jnp.where(
            fact == 0,
            total[h : h + 1],
            jnp.where(fact == 1, first_f, jnp.where(fact == 2, last_f, 0.0)),
        )
        for part in range(per_head):
            p = h * per_head + part
            pay_ref[p, 0:depth] = state[part * depth : (part + 1) * depth]
            pay_ref[p, depth : depth + META] = facts


def facts_of(fact_ref, j):
    return fact_ref[j, 0:1], fact_ref[j, 1:2], fact_ref[j, 2:3]


def summary(sum_ref, state, mark):
    depth = state.shape[0]
    row = lax.broadcasted_iota(jnp.int32, (META, state.shape[1]), 0)
    sum_ref[0:depth] = state
    sum_ref[depth : depth + META] = jnp.where(row == 1, mark, 0.0)


def forward_row(got_ref, sum_ref, fact_ref):
    depth = got_ref.shape[1] - META
    for j in range(ROW):
        fact_ref[j] = got_ref[j, depth : depth + META]
    state, mark = got_ref[0, 0:depth], facts_of(fact_ref, 0)[2]
    for j in range(1, ROW):
        decay, _, last = facts_of(fact_ref, j)
        state = jnp.where(mark == last, jnp.exp(decay), 0.0) * state + got_ref[j, 0:depth]
        mark = last
    summary(sum_ref, state, mark)


def backward_row(got_ref, fact_ref, sum_ref):
    state, mark = got_ref[ROW - 1], facts_of(fact_ref, ROW - 1)[1]
    for j in range(ROW - 2, -1, -1):
        decay, first, _ = facts_of(fact_ref, j)
        state = jnp.where(mark == first, jnp.exp(decay), 0.0) * state + got_ref[j]
        mark = first
    summary(sum_ref, state, mark)


def forward_scan(got_ref, fact_ref, near_ref, out_ref):
    depth = out_ref.shape[1]
    state, mark = near_ref[0:depth], near_ref[depth + 1 : depth + 2]
    for j in range(ROW):
        decay, first, last = facts_of(fact_ref, j)
        out_ref[j] = jnp.where(mark == first, state, 0.0)
        state = jnp.where(mark == last, jnp.exp(decay), 0.0) * state + got_ref[j, 0:depth]
        mark = last


def backward_scan(got_ref, fact_ref, near_ref, out_ref):
    depth = out_ref.shape[1]
    state, mark = near_ref[0:depth], near_ref[depth + 1 : depth + 2]
    for j in range(ROW - 1, -1, -1):
        decay, first, last = facts_of(fact_ref, j)
        out_ref[j] = jnp.where(mark == last, state, 0.0)
        state = jnp.where(mark == first, jnp.exp(decay), 0.0) * state + got_ref[j]
        mark = first


def decays_of(rows_ref, cols_ref, heads, h):
    tokens = cols_ref.shape[0]
    later = lax.broadcasted_iota(jnp.int32, (tokens, tokens), 0)
    earlier = lax.broadcasted_iota(jnp.int32, (tokens, tokens), 1)
    one = 3 * heads
    allowed = (cols_ref[:, one : one + 1] == rows_ref[one : one + 1]) & (later >= earlier)
    difference = cols_ref[:, h : h + 1] - rows_ref[h : h + 1]
    return jnp.where(allowed, jnp.exp(jnp.where(allowed, difference, 0.0)), 0.0)


def within_stretch(q_ref, k_ref, v_ref, rows_ref, cols_ref, scores_ref, within_ref):
    heads = q_ref.shape[0]
    for h in range(heads):
        decays = decays_of(rows_ref, cols_ref, heads, h)
        scores = (dot(q_ref[h], k_ref[h], 1, 1) * decays).astype(jnp.bfloat16)
        scores_ref[h] = scores
        within_ref[h] = dot(scores, v_ref[h], 1, 0)


def attend(q_ref, g_ref, state_ref, within_ref, cols_ref, att_ref, sums_ref):
    heads, tokens, width = q_ref.shape
    squares = crossed = jnp.zeros((tokens, width), jnp.float32)
    for h in range(heads):
        state = state_ref[h].astype(jnp.bfloat16)
        enter = cols_ref[:, heads + h : heads + h + 1]
        att = within_ref[h] + dot(q_ref[h], state, 1, 0) * enter
        att_ref[h] = att
        squares = squares + att * att
        crossed = crossed + g_ref[h].astype(jnp.float32) * att
    at = 0
    for terms in (squares, crossed):
        line = jnp.sum(terms.T, axis=0, keepdims=True)
        for start in range(0, tokens, width):
            piece = line[:, start : start + width]
            for p in range(sums_ref.shape[0]):
                sums_ref[p, at : at + 1] = piece
            at += 1


def normalise(features, q_ref, g_ref, att_ref, sums_ref, cols_ref, norm_ref, ga_ref, pay_ref, tmp_ref):
    heads, tokens, width = q_ref.shape
    per_head = ROW // heads
    depth = width // per_head
    lines = sums_ref.shape[1]
    tmp_ref[...] = jnp.zeros(tmp_ref.shape, jnp.float32)
    tmp_ref[0:lines] = jnp.sum(sums_ref[...], axis=0)
    upright = tmp_ref[...].T
    half = lines // 2
    squares = jnp.concatenate([upright[:, i : i + 1] for i in range(half)], axis=0)
    crossed = jnp.concatenate([upright[:, i : i + 1] for i in range(half, lines)], axis=0)
    mean = squares / features + EPSILON
    root = jnp.sqrt(mean)
    inverse = 1.0 / root
    factor = crossed / (features * root * root)
    for h in range(heads):
        att = att_ref[h]
        norm_ref[h] = (att * inverse).astype(jnp.bfloat16)
        ga = ((g_ref[h].astype(jnp.float32) - att * factor) * inverse).astype(jnp.bfloat16)
        ga_ref[h] = ga
        enter = cols_ref[:, heads + h : heads + h + 1]
        decayed = (q_ref[h].astype(jnp.float32) * enter).astype(jnp.bfloat16)
        back = dot(decayed, ga, 0, 0)
        for part in range(per_head):
            pay_ref[h * per_head + part] = back[part * depth : (part + 1) * depth]


def inner_gradients(
    q_ref, k_ref, v_ref, ga_ref, scores_ref, state_ref, rows_ref, cols_ref, gq_ref, ki_ref, vi_ref
):
    heads = q_ref.shape[0]
    for h in range(heads):
        ga = ga_ref[h]
        decays = decays_of(rows_ref, cols_ref, heads, h)
        slope = (dot(ga, v_ref[h], 1, 1) * decays).astype(jnp.bfloat16)
        enter = cols_ref[:, heads + h : heads + h + 1]
        state = state_ref[h].astype(jnp.bfloat16)
        gq_ref[h] = (dot(slope, k_ref[h], 1, 0) + dot(ga, state, 1, 1) * enter).astype(jnp.bfloat16)
        ki_ref[h] = dot(slope, q_ref[h], 0, 0)
        vi_ref[h] = dot(scores_ref[h], ga, 0, 0)


def outer_gradients(k_ref, v_ref, ki_ref, vi_ref, back_ref, cols_ref, gk_ref, gv_ref):
    heads = k_ref.shape[0]
    for h in range(heads):
        back = back_ref[h].astype(jnp.bfloat16)
        leave = cols_ref[:, 2 * heads + h : 2 * heads + h + 1]
        gk_ref[h] = (ki_ref[h] + dot(v_ref[h], back, 1, 1) * leave).astype(jnp.bfloat16)
        gv_ref[h] = (vi_ref[h] + dot(k_ref[h], back, 1, 0) * leave).astype(jnp.bfloat16)


def exchange(block, groups):
    return lax.all_to_all(
        block, "seq", split_axis=0, concat_axis=0, tiled=True, axis_index_groups=groups
    )


def passed_along(block, distance):
    devices = range(lax.axis_size("seq"))
    route = [(i, i + distance) for i in devices if i + distance in devices]
    return lax.ppermute(block, "seq", route)


def per_device(query_rows, key_rows, value_rows, log_gate, episode, grad_out):
    heads, tokens, width = query_rows.shape
    depth = heads * width // ROW
    devices = lax.axis_size("seq")
    groups = [list(range(at, at + ROW)) for at in range(0, devices, ROW)]
    f32, bf16 = jnp.float32, jnp.bfloat16
    block = (heads, tokens, width)
    product = 2 * heads * tokens * width * width
    square = 2 * heads * tokens * tokens * width
    line = 128

    pay, rows, cols = call(
        local_states,
        [
            ((ROW, depth + META, width), f32),
            ((line, tokens), f32),
            ((tokens, line), f32),
        ],
        product,
    )(log_gate, episode.reshape(1, tokens), key_rows, value_rows)
    got = exchange(pay, groups)
    total, facts = call(
        forward_row, [((depth + META, width), f32), ((ROW, META, width), f32)], got.size
    )(got)
    near = passed_along(total, ROW)
    scores, within = call(
        within_stretch, [((heads, tokens, tokens), bf16), (block, f32)], 2 * square
    )(query_rows, key_rows, value_rows, rows, cols)
    (states,) = call(forward_scan, [((ROW, depth, width), f32)], got.size)(got, facts, near)
    state = exchange(states, groups).reshape(heads, width, width)

    lines = 2 * tokens // width
    across = lax.axis_size("head")
    attention, sums = call(attend, [(block, f32), ((across, lines, width), f32)], product)(
        query_rows, grad_out, state, within, cols
    )
    sums = lax.all_to_all(sums, "head", split_axis=0, concat_axis=0, tiled=True)
    features = heads * across * width
    normed, grad_attn, pay = call(
        functools.partial(normalise, features),
        [(block, bf16), (block, bf16), ((ROW, depth, width), f32)],
        product,
        [pltpu.VMEM((width, width), f32)],
    )(query_rows, grad_out, attention, sums, cols)

    got = exchange(pay, groups)
    (total,) = call(backward_row, [((depth + META, width), f32)], got.size)(got, facts)
    near = passed_along(total, -ROW)
    query_grad, key_inner, value_inner = call(
        inner_gradients, [(block, bf16), (block, f32), (block, f32)], 4 * square + product
    )(query_rows, key_rows, value_rows, grad_attn, scores, state, rows, cols)
    (states,) = call(backward_scan, [((ROW, depth, width), f32)], got.size)(got, facts, near)
    back = exchange(states, groups).reshape(heads, width, width)
    key_grad, value_grad = call(outer_gradients, [(block, bf16), (block, bf16)], 2 * product)(
        key_rows, value_rows, key_inner, value_inner, back, cols
    )
    return normed, query_grad, key_grad, value_grad


def solution(mesh):
    rows = P("head", "seq", None)
    return jax.shard_map(
        per_device,
        mesh=mesh,
        in_specs=(rows, rows, rows, P("head", "seq"), P("seq"), rows),
        out_specs=(rows, rows, rows, rows),
        check_vma=False,
    )
```

```python
import functools

import jax
import jax.numpy as jnp
from jax import lax
from jax.experimental import pallas as pl
from jax.experimental.pallas import tpu as pltpu
from jax.sharding import PartitionSpec as P

EPSILON = 1e-06
ROW = 16
META = 8
HIGH = lax.Precision.HIGHEST


def dot(a, b, da, db):
    return lax.dot_general(
        a, b, (((da,), (db,)), ((), ())), preferred_element_type=jnp.float32
    )


def call(body, outs, flops, scratch=(), from_hbm=False, to_hbm=False):
    shapes = [jax.ShapeDtypeStruct(s, d) for s, d in outs]

    def run(*args):
        size = sum(a.size * a.dtype.itemsize for a in (*args, *shapes))
        return pl.pallas_call(
            body,
            out_shape=shapes,
            in_specs=[pl.BlockSpec(memory_space=pltpu.HBM if from_hbm else pltpu.VMEM)] * len(args),
            out_specs=[pl.BlockSpec(memory_space=pltpu.HBM if to_hbm else pltpu.VMEM)] * len(shapes),
            scratch_shapes=list(scratch),
            cost_estimate=pl.CostEstimate(flops=flops, bytes_accessed=size, transcendentals=0),
            compiler_params=pltpu.CompilerParams(vmem_limit_bytes=8 << 20),
            name=body.__name__ if hasattr(body, "__name__") else body.func.__name__,
        )(*args)

    return run


def local_states(
    gate_hbm, ep_hbm, k_hbm, v_hbm, pay_ref, rows_ref, cols_ref, gate_ref, ep_ref, k_ref, v_ref, sems
):
    heads, tokens = gate_ref.shape
    width = k_ref.shape[2]
    per_head = ROW // heads
    depth = width // per_head
    gates = pltpu.make_async_copy(gate_hbm, gate_ref, sems.at[0])
    ids = pltpu.make_async_copy(ep_hbm, ep_ref, sems.at[1])
    gates.start()
    ids.start()
    keys, values = [], []
    for h in range(heads):
        keys.append(pltpu.make_async_copy(k_hbm.at[h], k_ref.at[h], sems.at[2 + h]))
        values.append(pltpu.make_async_copy(v_hbm.at[h], v_ref.at[h], sems.at[2 + heads + h]))
        keys[h].start()
        values[h].start()
    gates.wait()
    run = gate_ref[...]
    place = lax.broadcasted_iota(jnp.int32, run.shape, 1)
    step = 1
    while step < tokens:
        run = run + jnp.where(place >= step, pltpu.roll(run, step, 1), 0.0)
        step *= 2
    total = run[:, tokens - 1 :]
    ids.wait()
    ep = ep_ref[...]
    first, last = ep[:, :1], ep[:, tokens - 1 :]
    rows_ref[...] = jnp.zeros(rows_ref.shape, jnp.float32)
    rows_ref[0:heads] = run
    rows_ref[heads : 2 * heads] = jnp.where(ep == first, jnp.exp(run), 0.0)
    rows_ref[2 * heads : 3 * heads] = jnp.where(ep == last, jnp.exp(total - run), 0.0)
    rows_ref[3 * heads : 3 * heads + 1] = ep.astype(jnp.float32)
    cols_ref[...] = rows_ref[...].T
    fact = lax.broadcasted_iota(jnp.int32, (META, width), 0)
    first_f, last_f = first.astype(jnp.float32), last.astype(jnp.float32)
    for h in range(heads):
        keys[h].wait()
        values[h].wait()
        leave = cols_ref[:, 2 * heads + h : 2 * heads + h + 1]
        decayed = (k_ref[h].astype(jnp.float32) * leave).astype(jnp.bfloat16)
        state = dot(decayed, v_ref[h], 0, 0)
        facts = jnp.where(
            fact == 0,
            total[h : h + 1],
            jnp.where(fact == 1, first_f, jnp.where(fact == 2, last_f, 0.0)),
        )
        for part in range(per_head):
            p = h * per_head + part
            pay_ref[p, 0:depth] = state[part * depth : (part + 1) * depth]
            pay_ref[p, depth : depth + META] = facts


def facts_of(fact_ref, j):
    return fact_ref[j, 0:1], fact_ref[j, 1:2], fact_ref[j, 2:3]


def summary(sum_ref, state, mark):
    depth = state.shape[0]
    row = lax.broadcasted_iota(jnp.int32, (META, state.shape[1]), 0)
    sum_ref[0:depth] = state
    sum_ref[depth : depth + META] = jnp.where(row == 1, mark, 0.0)


def forward_row(got_ref, sum_ref, fact_ref):
    depth = got_ref.shape[1] - META
    for j in range(ROW):
        fact_ref[j] = got_ref[j, depth : depth + META]
    state, mark = got_ref[0, 0:depth], facts_of(fact_ref, 0)[2]
    for j in range(1, ROW):
        decay, _, last = facts_of(fact_ref, j)
        state = jnp.where(mark == last, jnp.exp(decay), 0.0) * state + got_ref[j, 0:depth]
        mark = last
    summary(sum_ref, state, mark)


def backward_row(got_ref, fact_ref, sum_ref):
    state, mark = got_ref[ROW - 1], facts_of(fact_ref, ROW - 1)[1]
    for j in range(ROW - 2, -1, -1):
        decay, first, _ = facts_of(fact_ref, j)
        state = jnp.where(mark == first, jnp.exp(decay), 0.0) * state + got_ref[j]
        mark = first
    summary(sum_ref, state, mark)


def forward_scan(got_ref, fact_ref, near_ref, out_ref):
    depth = out_ref.shape[1]
    state, mark = near_ref[0:depth], near_ref[depth + 1 : depth + 2]
    for j in range(ROW):
        decay, first, last = facts_of(fact_ref, j)
        out_ref[j] = jnp.where(mark == first, state, 0.0)
        state = jnp.where(mark == last, jnp.exp(decay), 0.0) * state + got_ref[j, 0:depth]
        mark = last


def backward_scan(got_ref, fact_ref, near_ref, out_ref):
    depth = out_ref.shape[1]
    state, mark = near_ref[0:depth], near_ref[depth + 1 : depth + 2]
    for j in range(ROW - 1, -1, -1):
        decay, first, last = facts_of(fact_ref, j)
        out_ref[j] = jnp.where(mark == last, state, 0.0)
        state = jnp.where(mark == first, jnp.exp(decay), 0.0) * state + got_ref[j]
        mark = first


def decays_of(rows_ref, cols_ref, heads, h):
    tokens = cols_ref.shape[0]
    later = lax.broadcasted_iota(jnp.int32, (tokens, tokens), 0)
    earlier = lax.broadcasted_iota(jnp.int32, (tokens, tokens), 1)
    one = 3 * heads
    allowed = (cols_ref[:, one : one + 1] == rows_ref[one : one + 1]) & (later >= earlier)
    difference = cols_ref[:, h : h + 1] - rows_ref[h : h + 1]
    return jnp.where(allowed, jnp.exp(jnp.where(allowed, difference, 0.0)), 0.0)


def within_stretch(q_ref, k_ref, v_ref, rows_ref, cols_ref, scores_ref, within_ref):
    heads = q_ref.shape[0]
    for h in range(heads):
        decays = decays_of(rows_ref, cols_ref, heads, h)
        scores = (dot(q_ref[h], k_ref[h], 1, 1) * decays).astype(jnp.bfloat16)
        scores_ref[h] = scores
        within_ref[h] = dot(scores, v_ref[h], 1, 0)


def attend(q_ref, g_ref, state_ref, within_ref, cols_ref, att_ref, sums_ref):
    heads, tokens, width = q_ref.shape
    squares = crossed = jnp.zeros((tokens, width), jnp.float32)
    for h in range(heads):
        state = state_ref[h].astype(jnp.bfloat16)
        enter = cols_ref[:, heads + h : heads + h + 1]
        att = within_ref[h] + dot(q_ref[h], state, 1, 0) * enter
        att_ref[h] = att
        squares = squares + att * att
        crossed = crossed + g_ref[h].astype(jnp.float32) * att
    at = 0
    for terms in (squares, crossed):
        line = jnp.sum(terms.T, axis=0, keepdims=True)
        for start in range(0, tokens, width):
            piece = line[:, start : start + width]
            for p in range(sums_ref.shape[0]):
                sums_ref[p, at : at + 1] = piece
            at += 1


def token_scales(features, sums_ref, tmp_ref):
    lines = sums_ref.shape[1]
    tmp_ref[...] = jnp.zeros(tmp_ref.shape, jnp.float32)
    tmp_ref[0:lines] = jnp.sum(sums_ref[...], axis=0)
    upright = tmp_ref[...].T
    half = lines // 2
    squares = jnp.concatenate([upright[:, i : i + 1] for i in range(half)], axis=0)
    crossed = jnp.concatenate([upright[:, i : i + 1] for i in range(half, lines)], axis=0)
    root = jnp.sqrt(squares / features + EPSILON)
    return 1.0 / root, crossed / (features * root * root)


def own_gradient_state(
    features, q_ref, g_ref, att_ref, sums_ref, cols_ref, ga_ref, pay_ref, scale_ref, tmp_ref
):
    heads, tokens, width = q_ref.shape
    per_head = ROW // heads
    depth = width // per_head
    inverse, factor = token_scales(features, sums_ref, tmp_ref)
    scale_ref[...] = jnp.broadcast_to(inverse, scale_ref.shape)
    for h in range(heads):
        ga = ((g_ref[h].astype(jnp.float32) - att_ref[h] * factor) * inverse).astype(jnp.bfloat16)
        ga_ref[h] = ga
        enter = cols_ref[:, heads + h : heads + h + 1]
        decayed = (q_ref[h].astype(jnp.float32) * enter).astype(jnp.bfloat16)
        back = dot(decayed, ga, 0, 0)
        for part in range(per_head):
            pay_ref[h * per_head + part] = back[part * depth : (part + 1) * depth]


def inner_gradients(
    q_ref,
    k_ref,
    v_ref,
    ga_ref,
    scores_ref,
    state_ref,
    rows_ref,
    cols_ref,
    att_ref,
    scale_ref,
    norm_ref,
    gq_ref,
    ki_ref,
    vi_ref,
):
    heads = q_ref.shape[0]
    for h in range(heads):
        norm_ref[h] = (att_ref[h] * scale_ref[...]).astype(jnp.bfloat16)
        ga = ga_ref[h]
        decays = decays_of(rows_ref, cols_ref, heads, h)
        slope = (dot(ga, v_ref[h], 1, 1) * decays).astype(jnp.bfloat16)
        enter = cols_ref[:, heads + h : heads + h + 1]
        state = state_ref[h].astype(jnp.bfloat16)
        gq_ref[h] = (dot(slope, k_ref[h], 1, 0) + dot(ga, state, 1, 1) * enter).astype(jnp.bfloat16)
        ki_ref[h] = dot(slope, q_ref[h], 0, 0)
        vi_ref[h] = dot(scores_ref[h], ga, 0, 0)


def outer_gradients(
    k_ref, v_ref, ki_ref, vi_ref, back_ref, cols_ref, gk_hbm, gv_hbm, gk_ref, gv_ref, sems
):
    heads = k_ref.shape[0]
    copies = []
    for h in range(heads):
        back = back_ref[h].astype(jnp.bfloat16)
        leave = cols_ref[:, 2 * heads + h : 2 * heads + h + 1]
        gk_ref[h] = (ki_ref[h] + dot(v_ref[h], back, 1, 1) * leave).astype(jnp.bfloat16)
        copies.append(pltpu.make_async_copy(gk_ref.at[h], gk_hbm.at[h], sems.at[2 * h]))
        copies[-1].start()
        gv_ref[h] = (vi_ref[h] + dot(k_ref[h], back, 1, 0) * leave).astype(jnp.bfloat16)
        copies.append(pltpu.make_async_copy(gv_ref.at[h], gv_hbm.at[h], sems.at[2 * h + 1]))
        copies[-1].start()
    for copy in copies:
        copy.wait()


def in_hbm(array):
    return pltpu.with_memory_space_constraint(array, pltpu.HBM)


def exchange(block, groups):
    return lax.all_to_all(
        block, "seq", split_axis=0, concat_axis=0, tiled=True, axis_index_groups=groups
    )


def passed_along(block, distance):
    devices = range(lax.axis_size("seq"))
    route = [(i, i + distance) for i in devices if i + distance in devices]
    return lax.ppermute(block, "seq", route)


def per_device(query_rows, key_rows, value_rows, log_gate, episode, grad_out):
    heads, tokens, width = query_rows.shape
    depth = heads * width // ROW
    devices = lax.axis_size("seq")
    groups = [list(range(at, at + ROW)) for at in range(0, devices, ROW)]
    f32, bf16 = jnp.float32, jnp.bfloat16
    block = (heads, tokens, width)
    product = 2 * heads * tokens * width * width
    square = 2 * heads * tokens * tokens * width
    line = 128

    pay, rows, cols = call(
        local_states,
        [
            ((ROW, depth + META, width), f32),
            ((line, tokens), f32),
            ((tokens, line), f32),
        ],
        product,
        [
            pltpu.VMEM((heads, tokens), f32),
            pltpu.VMEM((1, tokens), jnp.int32),
            pltpu.VMEM(block, bf16),
            pltpu.VMEM(block, bf16),
            pltpu.SemaphoreType.DMA((2 + 2 * heads,)),
        ],
        from_hbm=True,
    )(*map(in_hbm, (log_gate, episode.reshape(1, tokens), key_rows, value_rows)))
    got = exchange(pay, groups)
    total, facts = call(
        forward_row, [((depth + META, width), f32), ((ROW, META, width), f32)], got.size
    )(got)
    near = passed_along(total, ROW)
    scores, within = call(
        within_stretch, [((heads, tokens, tokens), bf16), (block, f32)], 2 * square
    )(query_rows, key_rows, value_rows, rows, cols)
    near, scores, within = lax.optimization_barrier((near, scores, within))
    (states,) = call(forward_scan, [((ROW, depth, width), f32)], got.size)(got, facts, near)
    state = exchange(states, groups).reshape(heads, width, width)

    lines = 2 * tokens // width
    across = lax.axis_size("head")
    attention, sums = call(attend, [(block, f32), ((across, lines, width), f32)], product)(
        query_rows, grad_out, state, within, cols
    )
    sums = lax.all_to_all(sums, "head", split_axis=0, concat_axis=0, tiled=True)
    features = heads * across * width
    grad_attn, pay, scale = call(
        functools.partial(own_gradient_state, features),
        [(block, bf16), ((ROW, depth, width), f32), ((tokens, width), f32)],
        product,
        [pltpu.VMEM((width, width), f32)],
    )(query_rows, grad_out, attention, sums, cols)

    got = exchange(pay, groups)
    (total,) = call(backward_row, [((depth + META, width), f32)], got.size)(got, facts)
    near = passed_along(total, -ROW)
    normed, query_grad, key_inner, value_inner = call(
        inner_gradients,
        [(block, bf16), (block, bf16), (block, f32), (block, f32)],
        4 * square + product,
    )(
        query_rows,
        key_rows,
        value_rows,
        grad_attn,
        scores,
        state,
        rows,
        cols,
        attention,
        scale,
    )
    near, key_inner, value_inner = lax.optimization_barrier((near, key_inner, value_inner))
    (states,) = call(backward_scan, [((ROW, depth, width), f32)], got.size)(got, facts, near)
    back = exchange(states, groups).reshape(heads, width, width)
    key_grad, value_grad = call(
        outer_gradients,
        [(block, bf16), (block, bf16)],
        2 * product,
        [
            pltpu.VMEM(block, bf16),
            pltpu.VMEM(block, bf16),
            pltpu.SemaphoreType.DMA((2 * heads,)),
        ],
        to_hbm=True,
    )(key_rows, value_rows, key_inner, value_inner, back, cols)
    return normed, query_grad, key_grad, value_grad


def solution(mesh):
    rows = P("head", "seq", None)
    return jax.shard_map(
        per_device,
        mesh=mesh,
        in_specs=(rows, rows, rows, P("head", "seq"), P("seq"), rows),
        out_specs=(rows, rows, rows, rows),
        check_vma=False,
    )
```

```python
import functools

import jax
import jax.numpy as jnp
from jax import lax
from jax.experimental import pallas as pl
from jax.experimental.pallas import tpu as pltpu
from jax.sharding import PartitionSpec as P

EPSILON = 1e-06
ROW = 16
META = 8
HIGH = lax.Precision.HIGHEST


def dot(a, b, da, db):
    return lax.dot_general(
        a, b, (((da,), (db,)), ((), ())), preferred_element_type=jnp.float32
    )


def call(body, outs, flops, scratch=(), from_hbm=False, to_hbm=False):
    shapes = [jax.ShapeDtypeStruct(s, d) for s, d in outs]

    def run(*args):
        size = sum(a.size * a.dtype.itemsize for a in (*args, *shapes))
        return pl.pallas_call(
            body,
            out_shape=shapes,
            in_specs=[pl.BlockSpec(memory_space=pltpu.HBM if from_hbm else pltpu.VMEM)] * len(args),
            out_specs=[pl.BlockSpec(memory_space=pltpu.HBM if to_hbm else pltpu.VMEM)] * len(shapes),
            scratch_shapes=list(scratch),
            cost_estimate=pl.CostEstimate(flops=flops, bytes_accessed=size, transcendentals=0),
            compiler_params=pltpu.CompilerParams(vmem_limit_bytes=8 << 20),
            name=body.__name__ if hasattr(body, "__name__") else body.func.__name__,
        )(*args)

    return run


def running_sums(gates, ones):
    high = gates.astype(jnp.bfloat16)
    rest = gates - high.astype(jnp.float32)
    middle = rest.astype(jnp.bfloat16)
    low = (rest - middle.astype(jnp.float32)).astype(jnp.bfloat16)
    return dot(low, ones, 1, 0) + dot(middle, ones, 1, 0) + dot(high, ones, 1, 0)


def local_states(
    gate_hbm, ep_hbm, k_hbm, v_hbm, pay_ref, rows_ref, gate_ref, ep_ref, k_ref, v_ref, sems
):
    heads, tokens = gate_ref.shape
    width = k_ref.shape[2]
    per_head = ROW // heads
    depth = width // per_head
    gates = pltpu.make_async_copy(gate_hbm, gate_ref, sems.at[0])
    ids = pltpu.make_async_copy(ep_hbm, ep_ref, sems.at[1])
    gates.start()
    ids.start()
    keys = [pltpu.make_async_copy(k_hbm.at[h], k_ref.at[h], sems.at[2 + h]) for h in range(heads)]
    values = [
        pltpu.make_async_copy(v_hbm.at[h], v_ref.at[h], sems.at[2 + heads + h])
        for h in range(heads)
    ]
    for copy in (*keys, *values):
        copy.start()
    rows_ref[...] = jnp.zeros(rows_ref.shape, jnp.float32)
    upto = lax.broadcasted_iota(jnp.int32, (tokens, tokens), 0)
    place = lax.broadcasted_iota(jnp.int32, (tokens, tokens), 1)
    ones = jnp.where(upto <= place, 1.0, 0.0).astype(jnp.bfloat16)
    gates.wait()
    run = running_sums(gate_ref[...], ones)
    total = run[:, tokens - 1 :]
    ids.wait()
    ep = ep_ref[...]
    first, last = ep[:, :1], ep[:, tokens - 1 :]
    leave = jnp.where(ep == last, jnp.exp(total - run), 0.0)
    rows_ref[0:heads] = run
    rows_ref[heads : 2 * heads] = jnp.where(ep == first, jnp.exp(run), 0.0)
    rows_ref[2 * heads : 3 * heads] = leave
    rows_ref[3 * heads : 3 * heads + 1] = ep.astype(jnp.float32)
    fact = lax.broadcasted_iota(jnp.int32, (META, width), 0)
    first_f, last_f = first.astype(jnp.float32), last.astype(jnp.float32)
    for h in range(heads):
        keys[h].wait()
        decayed = (k_ref[h].T.astype(jnp.float32) * leave[h : h + 1]).astype(jnp.bfloat16)
        values[h].wait()
        state = dot(decayed, v_ref[h], 1, 0)
        facts = jnp.where(
            fact == 0,
            total[h : h + 1],
            jnp.where(fact == 1, first_f, jnp.where(fact == 2, last_f, 0.0)),
        )
        for part in range(per_head):
            p = h * per_head + part
            pay_ref[p, 0:depth] = state[part * depth : (part + 1) * depth]
            pay_ref[p, depth : depth + META] = facts


def facts_of(fact_ref, j):
    return fact_ref[j, 0:1], fact_ref[j, 1:2], fact_ref[j, 2:3]


def summary(sum_ref, state, mark):
    depth = state.shape[0]
    row = lax.broadcasted_iota(jnp.int32, (META, state.shape[1]), 0)
    sum_ref[0:depth] = state
    sum_ref[depth : depth + META] = jnp.where(row == 1, mark, 0.0)


def forward_row(got_ref, sum_ref, fact_ref):
    depth = got_ref.shape[1] - META
    for j in range(ROW):
        fact_ref[j] = got_ref[j, depth : depth + META]
    state, mark = got_ref[0, 0:depth], facts_of(fact_ref, 0)[2]
    for j in range(1, ROW):
        decay, _, last = facts_of(fact_ref, j)
        state = jnp.where(mark == last, jnp.exp(decay), 0.0) * state + got_ref[j, 0:depth]
        mark = last
    summary(sum_ref, state, mark)


def backward_row(got_ref, fact_ref, sum_ref):
    state, mark = got_ref[ROW - 1], facts_of(fact_ref, ROW - 1)[1]
    for j in range(ROW - 2, -1, -1):
        decay, first, _ = facts_of(fact_ref, j)
        state = jnp.where(mark == first, jnp.exp(decay), 0.0) * state + got_ref[j]
        mark = first
    summary(sum_ref, state, mark)


def forward_scan(got_ref, fact_ref, near_ref, out_ref):
    depth = out_ref.shape[1]
    state, mark = near_ref[0:depth], near_ref[depth + 1 : depth + 2]
    for j in range(ROW):
        decay, first, last = facts_of(fact_ref, j)
        out_ref[j] = jnp.where(mark == first, state, 0.0)
        state = jnp.where(mark == last, jnp.exp(decay), 0.0) * state + got_ref[j, 0:depth]
        mark = last


def backward_scan(got_ref, fact_ref, near_ref, out_ref):
    depth = out_ref.shape[1]
    state, mark = near_ref[0:depth], near_ref[depth + 1 : depth + 2]
    for j in range(ROW - 1, -1, -1):
        decay, first, last = facts_of(fact_ref, j)
        out_ref[j] = jnp.where(mark == last, state, 0.0)
        state = jnp.where(mark == first, jnp.exp(decay), 0.0) * state + got_ref[j]
        mark = first


def decays_of(rows_ref, cols_ref, heads, h):
    tokens = cols_ref.shape[0]
    later = lax.broadcasted_iota(jnp.int32, (tokens, tokens), 0)
    earlier = lax.broadcasted_iota(jnp.int32, (tokens, tokens), 1)
    one = 3 * heads
    allowed = (cols_ref[:, one : one + 1] == rows_ref[one : one + 1]) & (later >= earlier)
    difference = cols_ref[:, h : h + 1] - rows_ref[h : h + 1]
    return jnp.where(allowed, jnp.exp(jnp.where(allowed, difference, 0.0)), 0.0)


def within_stretch(
    q_ref, k_ref, v_ref, rows_ref, scores_ref, within_ref, decayed_ref, cols_ref
):
    heads = q_ref.shape[0]
    cols_ref[...] = rows_ref[...].T
    for h in range(heads):
        decays = decays_of(rows_ref, cols_ref, heads, h)
        scores = (dot(q_ref[h], k_ref[h], 1, 1) * decays).astype(jnp.bfloat16)
        scores_ref[h] = scores
        within_ref[h] = dot(scores, v_ref[h], 1, 0)
        enter = rows_ref[heads + h : heads + h + 1]
        decayed_ref[h] = (q_ref[h].astype(jnp.float32).T * enter).astype(jnp.bfloat16)


def attend(q_ref, g_ref, state_ref, within_ref, cols_ref, att_ref, sums_ref):
    heads, tokens, width = q_ref.shape
    squares = crossed = jnp.zeros((tokens, width), jnp.float32)
    for h in range(heads):
        state = state_ref[h].astype(jnp.bfloat16)
        enter = cols_ref[:, heads + h : heads + h + 1]
        att = within_ref[h] + dot(q_ref[h], state, 1, 0) * enter
        att_ref[h] = att
        squares = squares + att * att
        crossed = crossed + g_ref[h].astype(jnp.float32) * att
    at = 0
    for terms in (squares, crossed):
        line = jnp.sum(terms.T, axis=0, keepdims=True)
        for start in range(0, tokens, width):
            piece = line[:, start : start + width]
            for p in range(sums_ref.shape[0]):
                sums_ref[p, at : at + 1] = piece
            at += 1


def own_gradient_state(
    features, decayed_ref, g_ref, att_ref, sums_ref, ga_ref, pay_ref, scale_ref, tmp_ref
):
    heads, _, width = g_ref.shape
    per_head = ROW // heads
    depth = width // per_head
    half = sums_ref.shape[1] // 2
    sums = jnp.sum(sums_ref[...], axis=0)
    root = jnp.sqrt(sums[:half] / features + EPSILON)
    tmp_ref[0:half] = 1.0 / root
    tmp_ref[half : 2 * half] = sums[half:] / (features * root * root)
    upright = tmp_ref[...].T
    shape = scale_ref.shape
    inverse = jnp.concatenate([upright[:, i : i + 1] for i in range(half)], axis=0)
    factor = jnp.concatenate([upright[:, i : i + 1] for i in range(half, 2 * half)], axis=0)
    inverse, factor = jnp.broadcast_to(inverse, shape), jnp.broadcast_to(factor, shape)
    scale_ref[...] = inverse
    for h in range(heads):
        ga = ((g_ref[h].astype(jnp.float32) - att_ref[h] * factor) * inverse).astype(jnp.bfloat16)
        ga_ref[h] = ga
        back = dot(decayed_ref[h], ga, 1, 0)
        for part in range(per_head):
            pay_ref[h * per_head + part] = back[part * depth : (part + 1) * depth]


def inner_gradients(
    q_ref,
    k_ref,
    v_ref,
    ga_ref,
    scores_ref,
    state_ref,
    rows_ref,
    cols_ref,
    att_ref,
    scale_ref,
    norm_ref,
    gq_ref,
    ki_ref,
    vi_ref,
):
    heads = q_ref.shape[0]
    for h in range(heads):
        norm_ref[h] = (att_ref[h] * scale_ref[...]).astype(jnp.bfloat16)
        ga = ga_ref[h]
        decays = decays_of(rows_ref, cols_ref, heads, h)
        slope = (dot(ga, v_ref[h], 1, 1) * decays).astype(jnp.bfloat16)
        enter = cols_ref[:, heads + h : heads + h + 1]
        state = state_ref[h].astype(jnp.bfloat16)
        gq_ref[h] = (dot(slope, k_ref[h], 1, 0) + dot(ga, state, 1, 1) * enter).astype(jnp.bfloat16)
        ki_ref[h] = dot(slope, q_ref[h], 0, 0)
        vi_ref[h] = dot(scores_ref[h], ga, 0, 0)


def outer_gradients(
    k_ref, v_ref, ki_ref, vi_ref, back_ref, cols_ref, gk_hbm, gv_hbm, gk_ref, gv_ref, sems
):
    heads = k_ref.shape[0]
    copies = []
    for h in range(heads):
        back = back_ref[h].astype(jnp.bfloat16)
        leave = cols_ref[:, 2 * heads + h : 2 * heads + h + 1]
        gk_ref[h] = (ki_ref[h] + dot(v_ref[h], back, 1, 1) * leave).astype(jnp.bfloat16)
        copies.append(pltpu.make_async_copy(gk_ref.at[h], gk_hbm.at[h], sems.at[2 * h]))
        copies[-1].start()
        gv_ref[h] = (vi_ref[h] + dot(k_ref[h], back, 1, 0) * leave).astype(jnp.bfloat16)
        copies.append(pltpu.make_async_copy(gv_ref.at[h], gv_hbm.at[h], sems.at[2 * h + 1]))
        copies[-1].start()
    for copy in copies:
        copy.wait()


def in_hbm(array):
    return pltpu.with_memory_space_constraint(array, pltpu.HBM)


def exchange(block, groups):
    return lax.all_to_all(
        block, "seq", split_axis=0, concat_axis=0, tiled=True, axis_index_groups=groups
    )


def passed_along(block, distance):
    devices = range(lax.axis_size("seq"))
    route = [(i, i + distance) for i in devices if i + distance in devices]
    return lax.ppermute(block, "seq", route)


def per_device(query_rows, key_rows, value_rows, log_gate, episode, grad_out):
    heads, tokens, width = query_rows.shape
    depth = heads * width // ROW
    devices = lax.axis_size("seq")
    groups = [list(range(at, at + ROW)) for at in range(0, devices, ROW)]
    f32, bf16 = jnp.float32, jnp.bfloat16
    block = (heads, tokens, width)
    product = 2 * heads * tokens * width * width
    square = 2 * heads * tokens * tokens * width
    line = 128

    pay, rows = call(
        local_states,
        [
            ((ROW, depth + META, width), f32),
            ((line, tokens), f32),
        ],
        product,
        [
            pltpu.VMEM((heads, tokens), f32),
            pltpu.VMEM((1, tokens), jnp.int32),
            pltpu.VMEM(block, bf16),
            pltpu.VMEM(block, bf16),
            pltpu.SemaphoreType.DMA((2 + 2 * heads,)),
        ],
        from_hbm=True,
    )(*map(in_hbm, (log_gate, episode.reshape(1, tokens), key_rows, value_rows)))
    got = exchange(pay, groups)
    total, facts = call(
        forward_row, [((depth + META, width), f32), ((ROW, META, width), f32)], got.size
    )(got)
    near = passed_along(total, ROW)
    scores, within, decayed, cols = call(
        within_stretch,
        [
            ((heads, tokens, tokens), bf16),
            (block, f32),
            ((heads, width, tokens), bf16),
            ((tokens, line), f32),
        ],
        2 * square,
    )(query_rows, key_rows, value_rows, rows)
    near, within = lax.optimization_barrier((near, within))
    (states,) = call(forward_scan, [((ROW, depth, width), f32)], got.size)(got, facts, near)
    state = exchange(states, groups).reshape(heads, width, width)

    lines = 2 * tokens // width
    across = lax.axis_size("head")
    attention, sums = call(attend, [(block, f32), ((across, lines, width), f32)], product)(
        query_rows, grad_out, state, within, cols
    )
    sums = lax.all_to_all(sums, "head", split_axis=0, concat_axis=0, tiled=True)
    features = heads * across * width
    grad_attn, pay, scale = call(
        functools.partial(own_gradient_state, features),
        [(block, bf16), ((ROW, depth, width), f32), ((tokens, width), f32)],
        product,
        [pltpu.VMEM((8, width), f32)],
    )(decayed, grad_out, attention, sums)

    got = exchange(pay, groups)
    (total,) = call(backward_row, [((depth + META, width), f32)], got.size)(got, facts)
    near = passed_along(total, -ROW)
    normed, query_grad, key_inner, value_inner = call(
        inner_gradients,
        [(block, bf16), (block, bf16), (block, f32), (block, f32)],
        4 * square + product,
    )(
        query_rows,
        key_rows,
        value_rows,
        grad_attn,
        scores,
        state,
        rows,
        cols,
        attention,
        scale,
    )
    near, key_inner, value_inner = lax.optimization_barrier((near, key_inner, value_inner))
    (states,) = call(backward_scan, [((ROW, depth, width), f32)], got.size)(got, facts, near)
    back = exchange(states, groups).reshape(heads, width, width)
    key_grad, value_grad = call(
        outer_gradients,
        [(block, bf16), (block, bf16)],
        2 * product,
        [
            pltpu.VMEM(block, bf16),
            pltpu.VMEM(block, bf16),
            pltpu.SemaphoreType.DMA((2 * heads,)),
        ],
        to_hbm=True,
    )(key_rows, value_rows, key_inner, value_inner, back, cols)
    return normed, query_grad, key_grad, value_grad


def solution(mesh):
    rows = P("head", "seq", None)
    return jax.shard_map(
        per_device,
        mesh=mesh,
        in_specs=(rows, rows, rows, P("head", "seq"), P("seq"), rows),
        out_specs=(rows, rows, rows, rows),
        check_vma=False,
    )
```

```python
import functools

import jax
import jax.numpy as jnp
from jax import lax
from jax.experimental import pallas as pl
from jax.experimental.pallas import tpu as pltpu
from jax.sharding import PartitionSpec as P

EPSILON = 1e-06
ROW = 16
META = 8
HIGH = lax.Precision.HIGHEST


def dot(a, b, da, db):
    return lax.dot_general(
        a, b, (((da,), (db,)), ((), ())), preferred_element_type=jnp.float32
    )


def call(body, outs, flops, scratch=(), from_hbm=False, to_hbm=False):
    shapes = [jax.ShapeDtypeStruct(s, d) for s, d in outs]

    def run(*args):
        size = sum(a.size * a.dtype.itemsize for a in (*args, *shapes))
        return pl.pallas_call(
            body,
            out_shape=shapes,
            in_specs=[pl.BlockSpec(memory_space=pltpu.HBM if from_hbm else pltpu.VMEM)] * len(args),
            out_specs=[pl.BlockSpec(memory_space=pltpu.HBM if to_hbm else pltpu.VMEM)] * len(shapes),
            scratch_shapes=list(scratch),
            cost_estimate=pl.CostEstimate(flops=flops, bytes_accessed=size, transcendentals=0),
            compiler_params=pltpu.CompilerParams(vmem_limit_bytes=8 << 20),
            name=body.__name__ if hasattr(body, "__name__") else body.func.__name__,
        )(*args)

    return run


def running_sums(gates, ones):
    high = gates.astype(jnp.bfloat16)
    rest = gates - high.astype(jnp.float32)
    middle = rest.astype(jnp.bfloat16)
    low = (rest - middle.astype(jnp.float32)).astype(jnp.bfloat16)
    return dot(low, ones, 1, 0) + dot(middle, ones, 1, 0) + dot(high, ones, 1, 0)


def local_states(
    gate_hbm, ep_hbm, k_hbm, v_hbm, pay_ref, rows_ref, gate_ref, ep_ref, k_ref, v_ref, sems
):
    heads, tokens = gate_ref.shape
    width = k_ref.shape[2]
    per_head = ROW // heads
    depth = width // per_head
    gates = pltpu.make_async_copy(gate_hbm, gate_ref, sems.at[0])
    ids = pltpu.make_async_copy(ep_hbm, ep_ref, sems.at[1])
    gates.start()
    ids.start()
    keys = [pltpu.make_async_copy(k_hbm.at[h], k_ref.at[h], sems.at[2 + h]) for h in range(heads)]
    values = [
        pltpu.make_async_copy(v_hbm.at[h], v_ref.at[h], sems.at[2 + heads + h])
        for h in range(heads)
    ]
    for copy in (*keys, *values):
        copy.start()
    rows_ref[...] = jnp.zeros(rows_ref.shape, jnp.float32)
    upto = lax.broadcasted_iota(jnp.int32, (tokens, tokens), 0)
    place = lax.broadcasted_iota(jnp.int32, (tokens, tokens), 1)
    ones = jnp.where(upto <= place, 1.0, 0.0).astype(jnp.bfloat16)
    gates.wait()
    run = running_sums(gate_ref[...], ones)
    total = run[:, tokens - 1 :]
    ids.wait()
    ep = ep_ref[...]
    first, last = ep[:, :1], ep[:, tokens - 1 :]
    leave = jnp.where(ep == last, jnp.exp(total - run), 0.0)
    rows_ref[0:heads] = run
    rows_ref[heads : 2 * heads] = jnp.where(ep == first, jnp.exp(run), 0.0)
    rows_ref[2 * heads : 3 * heads] = leave
    rows_ref[3 * heads : 3 * heads + 1] = ep.astype(jnp.float32)
    fact = lax.broadcasted_iota(jnp.int32, (META, width), 0)
    first_f, last_f = first.astype(jnp.float32), last.astype(jnp.float32)
    for copy in (*keys, *values):
        copy.wait()
    for h in range(heads):
        decayed = (k_ref[h].T.astype(jnp.float32) * leave[h : h + 1]).astype(jnp.bfloat16)
        state = dot(decayed, v_ref[h], 1, 0)
        facts = jnp.where(
            fact == 0,
            total[h : h + 1],
            jnp.where(fact == 1, first_f, jnp.where(fact == 2, last_f, 0.0)),
        )
        for part in range(per_head):
            p = h * per_head + part
            pay_ref[p, 0:depth] = state[part * depth : (part + 1) * depth]
            pay_ref[p, depth : depth + META] = facts


def facts_of(fact_ref, j):
    return fact_ref[j, 0:1], fact_ref[j, 1:2], fact_ref[j, 2:3]


def summary(sum_ref, state, mark):
    depth = state.shape[0]
    row = lax.broadcasted_iota(jnp.int32, (META, state.shape[1]), 0)
    sum_ref[0:depth] = state
    sum_ref[depth : depth + META] = jnp.where(row == 1, mark, 0.0)


def forward_row(got_ref, sum_ref, fact_ref):
    depth = got_ref.shape[1] - META
    for j in range(ROW):
        fact_ref[j] = got_ref[j, depth : depth + META]
    state, mark = got_ref[0, 0:depth], facts_of(fact_ref, 0)[2]
    for j in range(1, ROW):
        decay, _, last = facts_of(fact_ref, j)
        state = jnp.where(mark == last, jnp.exp(decay), 0.0) * state + got_ref[j, 0:depth]
        mark = last
    summary(sum_ref, state, mark)


def backward_row(got_ref, fact_ref, sum_ref):
    state, mark = got_ref[ROW - 1], facts_of(fact_ref, ROW - 1)[1]
    for j in range(ROW - 2, -1, -1):
        decay, first, _ = facts_of(fact_ref, j)
        state = jnp.where(mark == first, jnp.exp(decay), 0.0) * state + got_ref[j]
        mark = first
    summary(sum_ref, state, mark)


def forward_scan(got_ref, fact_ref, near_ref, out_ref):
    depth = out_ref.shape[1]
    state, mark = near_ref[0:depth], near_ref[depth + 1 : depth + 2]
    for j in range(ROW):
        decay, first, last = facts_of(fact_ref, j)
        out_ref[j] = jnp.where(mark == first, state, 0.0)
        state = jnp.where(mark == last, jnp.exp(decay), 0.0) * state + got_ref[j, 0:depth]
        mark = last


def backward_scan(got_ref, fact_ref, near_ref, out_ref):
    depth = out_ref.shape[1]
    state, mark = near_ref[0:depth], near_ref[depth + 1 : depth + 2]
    for j in range(ROW - 1, -1, -1):
        decay, first, last = facts_of(fact_ref, j)
        out_ref[j] = jnp.where(mark == last, state, 0.0)
        state = jnp.where(mark == first, jnp.exp(decay), 0.0) * state + got_ref[j]
        mark = first


def decays_of(rows_ref, cols_ref, heads, h):
    tokens = cols_ref.shape[0]
    later = lax.broadcasted_iota(jnp.int32, (tokens, tokens), 0)
    earlier = lax.broadcasted_iota(jnp.int32, (tokens, tokens), 1)
    one = 3 * heads
    allowed = (cols_ref[:, one : one + 1] == rows_ref[one : one + 1]) & (later >= earlier)
    difference = cols_ref[:, h : h + 1] - rows_ref[h : h + 1]
    return jnp.where(allowed, jnp.exp(jnp.where(allowed, difference, 0.0)), 0.0)


def within_stretch(
    q_ref, k_ref, v_ref, rows_ref, scores_ref, within_ref, decayed_ref, cols_ref
):
    heads = q_ref.shape[0]
    cols_ref[...] = rows_ref[...].T
    for h in range(heads):
        decays = decays_of(rows_ref, cols_ref, heads, h)
        scores = (dot(q_ref[h], k_ref[h], 1, 1) * decays).astype(jnp.bfloat16)
        scores_ref[h] = scores
        within_ref[h] = dot(scores, v_ref[h], 1, 0)
        enter = rows_ref[heads + h : heads + h + 1]
        decayed_ref[h] = (q_ref[h].astype(jnp.float32).T * enter).astype(jnp.bfloat16)


def attend(q_ref, g_ref, state_ref, within_ref, cols_ref, att_ref, sums_ref):
    heads, tokens, width = q_ref.shape
    squares = crossed = jnp.zeros((tokens, width), jnp.float32)
    for h in range(heads):
        state = state_ref[h].astype(jnp.bfloat16)
        enter = cols_ref[:, heads + h : heads + h + 1]
        att = within_ref[h] + dot(q_ref[h], state, 1, 0) * enter
        att_ref[h] = att
        squares = squares + att * att
        crossed = crossed + g_ref[h].astype(jnp.float32) * att
    at = 0
    for terms in (squares, crossed):
        line = jnp.sum(terms.T, axis=0, keepdims=True)
        for start in range(0, tokens, width):
            piece = line[:, start : start + width]
            for p in range(sums_ref.shape[0]):
                sums_ref[p, at : at + 1] = piece
            at += 1


def own_gradient_state(
    features, decayed_ref, g_ref, att_ref, sums_ref, ga_ref, pay_ref, scale_ref, tmp_ref
):
    heads, _, width = g_ref.shape
    per_head = ROW // heads
    depth = width // per_head
    half = sums_ref.shape[1] // 2
    sums = jnp.sum(sums_ref[...], axis=0)
    root = jnp.sqrt(sums[:half] / features + EPSILON)
    tmp_ref[0:half] = 1.0 / root
    tmp_ref[half : 2 * half] = sums[half:] / (features * root * root)
    upright = tmp_ref[...].T
    shape = scale_ref.shape
    inverse = jnp.concatenate([upright[:, i : i + 1] for i in range(half)], axis=0)
    factor = jnp.concatenate([upright[:, i : i + 1] for i in range(half, 2 * half)], axis=0)
    inverse, factor = jnp.broadcast_to(inverse, shape), jnp.broadcast_to(factor, shape)
    scale_ref[...] = inverse
    for h in range(heads):
        ga = ((g_ref[h].astype(jnp.float32) - att_ref[h] * factor) * inverse).astype(jnp.bfloat16)
        ga_ref[h] = ga
        back = dot(decayed_ref[h], ga, 1, 0)
        for part in range(per_head):
            pay_ref[h * per_head + part] = back[part * depth : (part + 1) * depth]


def inner_gradients(
    q_ref,
    k_ref,
    v_ref,
    ga_ref,
    scores_ref,
    state_ref,
    rows_ref,
    cols_ref,
    att_ref,
    scale_ref,
    norm_ref,
    gq_ref,
    ki_ref,
    vi_ref,
):
    heads = q_ref.shape[0]
    for h in range(heads):
        norm_ref[h] = (att_ref[h] * scale_ref[...]).astype(jnp.bfloat16)
        ga = ga_ref[h]
        decays = decays_of(rows_ref, cols_ref, heads, h)
        slope = (dot(ga, v_ref[h], 1, 1) * decays).astype(jnp.bfloat16)
        enter = cols_ref[:, heads + h : heads + h + 1]
        state = state_ref[h].astype(jnp.bfloat16)
        gq_ref[h] = (dot(slope, k_ref[h], 1, 0) + dot(ga, state, 1, 1) * enter).astype(jnp.bfloat16)
        ki_ref[h] = dot(slope, q_ref[h], 0, 0)
        vi_ref[h] = dot(scores_ref[h], ga, 0, 0)


def outer_gradients(
    k_ref, v_ref, ki_ref, vi_ref, back_ref, cols_ref, gk_hbm, gv_hbm, gk_ref, gv_ref, sems
):
    heads = k_ref.shape[0]
    copies = []
    for h in range(heads):
        back = back_ref[h].astype(jnp.bfloat16)
        leave = cols_ref[:, 2 * heads + h : 2 * heads + h + 1]
        gk_ref[h] = (ki_ref[h] + dot(v_ref[h], back, 1, 1) * leave).astype(jnp.bfloat16)
        copies.append(pltpu.make_async_copy(gk_ref.at[h], gk_hbm.at[h], sems.at[2 * h]))
        copies[-1].start()
        gv_ref[h] = (vi_ref[h] + dot(k_ref[h], back, 1, 0) * leave).astype(jnp.bfloat16)
        copies.append(pltpu.make_async_copy(gv_ref.at[h], gv_hbm.at[h], sems.at[2 * h + 1]))
        copies[-1].start()
    for copy in copies:
        copy.wait()


def in_hbm(array):
    return pltpu.with_memory_space_constraint(array, pltpu.HBM)


def exchange(block, groups):
    return lax.all_to_all(
        block, "seq", split_axis=0, concat_axis=0, tiled=True, axis_index_groups=groups
    )


def passed_along(block, distance):
    devices = range(lax.axis_size("seq"))
    route = [(i, i + distance) for i in devices if i + distance in devices]
    return lax.ppermute(block, "seq", route)


def per_device(query_rows, key_rows, value_rows, log_gate, episode, grad_out):
    heads, tokens, width = query_rows.shape
    depth = heads * width // ROW
    devices = lax.axis_size("seq")
    groups = [list(range(at, at + ROW)) for at in range(0, devices, ROW)]
    f32, bf16 = jnp.float32, jnp.bfloat16
    block = (heads, tokens, width)
    product = 2 * heads * tokens * width * width
    square = 2 * heads * tokens * tokens * width
    line = 128

    pay, rows = call(
        local_states,
        [
            ((ROW, depth + META, width), f32),
            ((line, tokens), f32),
        ],
        product,
        [
            pltpu.VMEM((heads, tokens), f32),
            pltpu.VMEM((1, tokens), jnp.int32),
            pltpu.VMEM(block, bf16),
            pltpu.VMEM(block, bf16),
            pltpu.SemaphoreType.DMA((2 + 2 * heads,)),
        ],
        from_hbm=True,
    )(*map(in_hbm, (log_gate, episode.reshape(1, tokens), key_rows, value_rows)))
    got = exchange(pay, groups)
    total, facts = call(
        forward_row, [((depth + META, width), f32), ((ROW, META, width), f32)], got.size
    )(got)
    near = passed_along(total, ROW)
    scores, within, decayed, cols = call(
        within_stretch,
        [
            ((heads, tokens, tokens), bf16),
            (block, f32),
            ((heads, width, tokens), bf16),
            ((tokens, line), f32),
        ],
        2 * square,
    )(query_rows, key_rows, value_rows, rows)
    near, within = lax.optimization_barrier((near, within))
    (states,) = call(forward_scan, [((ROW, depth, width), f32)], got.size)(got, facts, near)
    state = exchange(states, groups).reshape(heads, width, width)

    lines = 2 * tokens // width
    across = lax.axis_size("head")
    attention, sums = call(attend, [(block, f32), ((across, lines, width), f32)], product)(
        query_rows, grad_out, state, within, cols
    )
    sums = lax.all_to_all(sums, "head", split_axis=0, concat_axis=0, tiled=True)
    features = heads * across * width
    grad_attn, pay, scale = call(
        functools.partial(own_gradient_state, features),
        [(block, bf16), ((ROW, depth, width), f32), ((tokens, width), f32)],
        product,
        [pltpu.VMEM((8, width), f32)],
    )(decayed, grad_out, attention, sums)

    got = exchange(pay, groups)
    (total,) = call(backward_row, [((depth + META, width), f32)], got.size)(got, facts)
    near = passed_along(total, -ROW)
    normed, query_grad, key_inner, value_inner = call(
        inner_gradients,
        [(block, bf16), (block, bf16), (block, f32), (block, f32)],
        4 * square + product,
    )(
        query_rows,
        key_rows,
        value_rows,
        grad_attn,
        scores,
        state,
        rows,
        cols,
        attention,
        scale,
    )
    near, key_inner, value_inner = lax.optimization_barrier((near, key_inner, value_inner))
    (states,) = call(backward_scan, [((ROW, depth, width), f32)], got.size)(got, facts, near)
    back = exchange(states, groups).reshape(heads, width, width)
    key_grad, value_grad = call(
        outer_gradients,
        [(block, bf16), (block, bf16)],
        2 * product,
        [
            pltpu.VMEM(block, bf16),
            pltpu.VMEM(block, bf16),
            pltpu.SemaphoreType.DMA((2 * heads,)),
        ],
        to_hbm=True,
    )(key_rows, value_rows, key_inner, value_inner, back, cols)
    return normed, query_grad, key_grad, value_grad


def solution(mesh):
    rows = P("head", "seq", None)
    return jax.shard_map(
        per_device,
        mesh=mesh,
        in_specs=(rows, rows, rows, P("head", "seq"), P("seq"), rows),
        out_specs=(rows, rows, rows, rows),
        check_vma=False,
    )
```

```python
import functools

import jax
import jax.numpy as jnp
from jax import lax
from jax.experimental import pallas as pl
from jax.experimental.pallas import tpu as pltpu
from jax.sharding import PartitionSpec as P

EPSILON = 1e-06
ROW = 16
LEAD = 4
META = 8
HIGH = lax.Precision.HIGHEST


def dot(a, b, da, db):
    return lax.dot_general(
        a, b, (((da,), (db,)), ((), ())), preferred_element_type=jnp.float32
    )


def listed():
    lead = jnp.where(lax.axis_index("seq") < ROW, 0, LEAD)
    return lambda member: lax.rem(member + ROW - lead, ROW)


def call(body, outs, flops, scratch=(), from_hbm=False, to_hbm=False):
    shapes = [jax.ShapeDtypeStruct(s, d) for s, d in outs]

    def run(*args):
        size = sum(a.size * a.dtype.itemsize for a in (*args, *shapes))
        return pl.pallas_call(
            body,
            out_shape=shapes,
            in_specs=[pl.BlockSpec(memory_space=pltpu.HBM if from_hbm else pltpu.VMEM)] * len(args),
            out_specs=[pl.BlockSpec(memory_space=pltpu.HBM if to_hbm else pltpu.VMEM)] * len(shapes),
            scratch_shapes=list(scratch),
            cost_estimate=pl.CostEstimate(flops=flops, bytes_accessed=size, transcendentals=0),
            compiler_params=pltpu.CompilerParams(vmem_limit_bytes=8 << 20),
            name=body.__name__ if hasattr(body, "__name__") else body.func.__name__,
        )(*args)

    return run


def running_sums(gates, ones):
    high = gates.astype(jnp.bfloat16)
    rest = gates - high.astype(jnp.float32)
    middle = rest.astype(jnp.bfloat16)
    low = (rest - middle.astype(jnp.float32)).astype(jnp.bfloat16)
    return dot(low, ones, 1, 0) + dot(middle, ones, 1, 0) + dot(high, ones, 1, 0)


def local_states(
    gate_hbm, ep_hbm, k_hbm, v_hbm, pay_ref, rows_ref, gate_ref, ep_ref, k_ref, v_ref, sems
):
    heads, tokens = gate_ref.shape
    width = k_ref.shape[2]
    per_head = ROW // heads
    depth = width // per_head
    slot = listed()
    gates = pltpu.make_async_copy(gate_hbm, gate_ref, sems.at[0])
    ids = pltpu.make_async_copy(ep_hbm, ep_ref, sems.at[1])
    gates.start()
    ids.start()
    keys = [pltpu.make_async_copy(k_hbm.at[h], k_ref.at[h], sems.at[2 + h]) for h in range(heads)]
    values = [
        pltpu.make_async_copy(v_hbm.at[h], v_ref.at[h], sems.at[2 + heads + h])
        for h in range(heads)
    ]
    for copy in (*keys, *values):
        copy.start()
    rows_ref[...] = jnp.zeros(rows_ref.shape, jnp.float32)
    upto = lax.broadcasted_iota(jnp.int32, (tokens, tokens), 0)
    place = lax.broadcasted_iota(jnp.int32, (tokens, tokens), 1)
    ones = jnp.where(upto <= place, 1.0, 0.0).astype(jnp.bfloat16)
    gates.wait()
    run = running_sums(gate_ref[...], ones)
    total = run[:, tokens - 1 :]
    ids.wait()
    ep = ep_ref[...]
    first, last = ep[:, :1], ep[:, tokens - 1 :]
    leave = jnp.where(ep == last, jnp.exp(total - run), 0.0)
    rows_ref[0:heads] = run
    rows_ref[heads : 2 * heads] = jnp.where(ep == first, jnp.exp(run), 0.0)
    rows_ref[2 * heads : 3 * heads] = leave
    rows_ref[3 * heads : 3 * heads + 1] = ep.astype(jnp.float32)
    fact = lax.broadcasted_iota(jnp.int32, (1, width), 1)
    first_f, last_f = first.astype(jnp.float32), last.astype(jnp.float32)
    for copy in (*keys, *values):
        copy.wait()
    for h in range(heads):
        decayed = (k_ref[h].T.astype(jnp.float32) * leave[h : h + 1]).astype(jnp.bfloat16)
        state = dot(decayed, v_ref[h], 1, 0)
        facts = jnp.where(
            fact == 0,
            total[h : h + 1],
            jnp.where(fact == 1, first_f, jnp.where(fact == 2, last_f, 0.0)),
        )
        for part in range(per_head):
            at = slot(h * per_head + part) * (depth + 1)
            pay_ref[pl.ds(at, depth)] = state[part * depth : (part + 1) * depth]
            pay_ref[pl.ds(at + depth, 1)] = facts


def facts_of(fact_ref, j):
    return fact_ref[j, 0:1], fact_ref[j, 1:2], fact_ref[j, 2:3]


def summary(sum_ref, state, mark):
    depth = state.shape[0]
    row = lax.broadcasted_iota(jnp.int32, (META, state.shape[1]), 0)
    sum_ref[0:depth] = state
    sum_ref[depth : depth + META] = jnp.where(row == 1, mark, 0.0)


def forward_row(got_ref, sum_ref, fact_ref):
    stride = got_ref.shape[0] // ROW
    depth, shape = stride - 1, (1, got_ref.shape[1])
    slot = listed()
    for j in range(ROW):
        facts = got_ref[pl.ds(slot(j) * stride + depth, 1)]
        for i in range(3):
            fact_ref[j, i : i + 1] = jnp.broadcast_to(facts[:, i : i + 1], shape)
    state, mark = got_ref[pl.ds(slot(0) * stride, depth)], facts_of(fact_ref, 0)[2]
    for j in range(1, ROW):
        decay, _, last = facts_of(fact_ref, j)
        kept = jnp.where(mark == last, jnp.exp(decay), 0.0)
        state = kept * state + got_ref[pl.ds(slot(j) * stride, depth)]
        mark = last
    summary(sum_ref, state, mark)


def backward_row(got_ref, fact_ref, sum_ref):
    slot = listed()
    state, mark = got_ref[slot(ROW - 1)], facts_of(fact_ref, ROW - 1)[1]
    for j in range(ROW - 2, -1, -1):
        decay, first, _ = facts_of(fact_ref, j)
        state = jnp.where(mark == first, jnp.exp(decay), 0.0) * state + got_ref[slot(j)]
        mark = first
    summary(sum_ref, state, mark)


def forward_scan(got_ref, fact_ref, near_ref, out_ref):
    depth = out_ref.shape[1]
    slot = listed()
    state, mark = near_ref[0:depth], near_ref[depth + 1 : depth + 2]
    for j in range(ROW):
        decay, first, last = facts_of(fact_ref, j)
        out_ref[slot(j)] = jnp.where(mark == first, state, 0.0)
        kept = jnp.where(mark == last, jnp.exp(decay), 0.0)
        state = kept * state + got_ref[pl.ds(slot(j) * (depth + 1), depth)]
        mark = last


def backward_scan(got_ref, fact_ref, near_ref, out_ref):
    depth = out_ref.shape[1]
    slot = listed()
    state, mark = near_ref[0:depth], near_ref[depth + 1 : depth + 2]
    for j in range(ROW - 1, -1, -1):
        decay, first, last = facts_of(fact_ref, j)
        out_ref[slot(j)] = jnp.where(mark == last, state, 0.0)
        state = jnp.where(mark == first, jnp.exp(decay), 0.0) * state + got_ref[slot(j)]
        mark = first


def head_state(state_ref, slot, heads, h):
    per_head = ROW // heads
    slices = [state_ref[slot(h * per_head + part)] for part in range(per_head)]
    return jnp.concatenate(slices, axis=0).astype(jnp.bfloat16)


def decays_of(rows_ref, cols_ref, heads, h):
    tokens = cols_ref.shape[0]
    later = lax.broadcasted_iota(jnp.int32, (tokens, tokens), 0)
    earlier = lax.broadcasted_iota(jnp.int32, (tokens, tokens), 1)
    one = 3 * heads
    allowed = (cols_ref[:, one : one + 1] == rows_ref[one : one + 1]) & (later >= earlier)
    difference = cols_ref[:, h : h + 1] - rows_ref[h : h + 1]
    return jnp.where(allowed, jnp.exp(jnp.where(allowed, difference, 0.0)), 0.0)


def within_stretch(
    q_ref, k_ref, v_ref, rows_ref, scores_ref, within_ref, decayed_ref, cols_ref
):
    heads = q_ref.shape[0]
    cols_ref[...] = rows_ref[...].T
    for h in range(heads):
        decays = decays_of(rows_ref, cols_ref, heads, h)
        scores = (dot(q_ref[h], k_ref[h], 1, 1) * decays).astype(jnp.bfloat16)
        scores_ref[h] = scores
        within_ref[h] = dot(scores, v_ref[h], 1, 0)
        enter = rows_ref[heads + h : heads + h + 1]
        decayed_ref[h] = (q_ref[h].astype(jnp.float32).T * enter).astype(jnp.bfloat16)


def attend(q_ref, g_ref, state_ref, within_ref, cols_ref, att_ref, sums_ref):
    heads, tokens, width = q_ref.shape
    slot = listed()
    squares = crossed = jnp.zeros((tokens, width), jnp.float32)
    for h in range(heads):
        state = head_state(state_ref, slot, heads, h)
        enter = cols_ref[:, heads + h : heads + h + 1]
        att = within_ref[h] + dot(q_ref[h], state, 1, 0) * enter
        att_ref[h] = att
        squares = squares + att * att
        crossed = crossed + g_ref[h].astype(jnp.float32) * att
    at = 0
    for terms in (squares, crossed):
        line = jnp.sum(terms.T, axis=0, keepdims=True)
        for start in range(0, tokens, width):
            piece = line[:, start : start + width]
            for p in range(sums_ref.shape[0]):
                sums_ref[p, at : at + 1] = piece
            at += 1


def own_gradient_state(
    features, decayed_ref, g_ref, att_ref, sums_ref, ga_ref, pay_ref, scale_ref, tmp_ref
):
    heads, _, width = g_ref.shape
    per_head = ROW // heads
    depth = width // per_head
    slot = listed()
    half = sums_ref.shape[1] // 2
    sums = jnp.sum(sums_ref[...], axis=0)
    root = jnp.sqrt(sums[:half] / features + EPSILON)
    tmp_ref[0:half] = 1.0 / root
    tmp_ref[half : 2 * half] = sums[half:] / (features * root * root)
    upright = tmp_ref[...].T
    shape = scale_ref.shape
    inverse = jnp.concatenate([upright[:, i : i + 1] for i in range(half)], axis=0)
    factor = jnp.concatenate([upright[:, i : i + 1] for i in range(half, 2 * half)], axis=0)
    inverse, factor = jnp.broadcast_to(inverse, shape), jnp.broadcast_to(factor, shape)
    scale_ref[...] = inverse
    for h in range(heads):
        ga = ((g_ref[h].astype(jnp.float32) - att_ref[h] * factor) * inverse).astype(jnp.bfloat16)
        ga_ref[h] = ga
        back = dot(decayed_ref[h], ga, 1, 0)
        for part in range(per_head):
            pay_ref[slot(h * per_head + part)] = back[part * depth : (part + 1) * depth]


def inner_gradients(
    q_ref,
    k_ref,
    v_ref,
    ga_ref,
    scores_ref,
    state_ref,
    rows_ref,
    cols_ref,
    att_ref,
    scale_ref,
    norm_ref,
    gq_ref,
    ki_ref,
    vi_ref,
):
    heads = q_ref.shape[0]
    slot = listed()
    for h in range(heads):
        norm_ref[h] = (att_ref[h] * scale_ref[...]).astype(jnp.bfloat16)
        ga = ga_ref[h]
        decays = decays_of(rows_ref, cols_ref, heads, h)
        slope = (dot(ga, v_ref[h], 1, 1) * decays).astype(jnp.bfloat16)
        enter = cols_ref[:, heads + h : heads + h + 1]
        state = head_state(state_ref, slot, heads, h)
        gq_ref[h] = (dot(slope, k_ref[h], 1, 0) + dot(ga, state, 1, 1) * enter).astype(jnp.bfloat16)
        ki_ref[h] = dot(slope, q_ref[h], 0, 0)
        vi_ref[h] = dot(scores_ref[h], ga, 0, 0)


def outer_gradients(
    k_ref, v_ref, ki_ref, vi_ref, back_ref, cols_ref, gk_hbm, gv_hbm, gk_ref, gv_ref, sems
):
    heads = k_ref.shape[0]
    slot = listed()
    copies = []
    for h in range(heads):
        back = head_state(back_ref, slot, heads, h)
        leave = cols_ref[:, 2 * heads + h : 2 * heads + h + 1]
        gk_ref[h] = (ki_ref[h] + dot(v_ref[h], back, 1, 1) * leave).astype(jnp.bfloat16)
        copies.append(pltpu.make_async_copy(gk_ref.at[h], gk_hbm.at[h], sems.at[2 * h]))
        copies[-1].start()
        gv_ref[h] = (vi_ref[h] + dot(k_ref[h], back, 1, 0) * leave).astype(jnp.bfloat16)
        copies.append(pltpu.make_async_copy(gv_ref.at[h], gv_hbm.at[h], sems.at[2 * h + 1]))
        copies[-1].start()
    for copy in copies:
        copy.wait()


def in_hbm(array):
    return pltpu.with_memory_space_constraint(array, pltpu.HBM)


def exchange(block, groups):
    return lax.all_to_all(
        block, "seq", split_axis=0, concat_axis=0, tiled=True, axis_index_groups=groups
    )


def passed_along(block, distance):
    devices = range(lax.axis_size("seq"))
    route = [(i, i + distance) for i in devices if i + distance in devices]
    return lax.ppermute(block, "seq", route)


def per_device(query_rows, key_rows, value_rows, log_gate, episode, grad_out):
    heads, tokens, width = query_rows.shape
    depth = heads * width // ROW
    devices = lax.axis_size("seq")
    groups = [
        [at + (i + (LEAD if at else 0)) % ROW for i in range(ROW)] for at in range(0, devices, ROW)
    ]
    f32, bf16 = jnp.float32, jnp.bfloat16
    block = (heads, tokens, width)
    product = 2 * heads * tokens * width * width
    square = 2 * heads * tokens * tokens * width
    line = 128

    pay, rows = call(
        local_states,
        [
            ((ROW * (depth + 1), width), f32),
            ((line, tokens), f32),
        ],
        product,
        [
            pltpu.VMEM((heads, tokens), f32),
            pltpu.VMEM((1, tokens), jnp.int32),
            pltpu.VMEM(block, bf16),
            pltpu.VMEM(block, bf16),
            pltpu.SemaphoreType.DMA((2 + 2 * heads,)),
        ],
        from_hbm=True,
    )(*map(in_hbm, (log_gate, episode.reshape(1, tokens), key_rows, value_rows)))
    dense = (ROW, depth + 1, 1, width)
    got = exchange(pay.reshape(dense), groups).reshape(pay.shape)
    total, facts = call(
        forward_row, [((depth + META, width), f32), ((ROW, META, width), f32)], got.size
    )(got)
    near = passed_along(total, ROW)
    scores, within, decayed, cols = call(
        within_stretch,
        [
            ((heads, tokens, tokens), bf16),
            (block, f32),
            ((heads, width, tokens), bf16),
            ((tokens, line), f32),
        ],
        2 * square,
    )(query_rows, key_rows, value_rows, rows)
    near, within = lax.optimization_barrier((near, within))
    (states,) = call(forward_scan, [((ROW, depth, width), f32)], got.size)(got, facts, near)
    state = exchange(states, groups)

    lines = 2 * tokens // width
    across = lax.axis_size("head")
    attention, sums = call(attend, [(block, f32), ((across, lines, width), f32)], product)(
        query_rows, grad_out, state, within, cols
    )
    sums = lax.all_to_all(sums, "head", split_axis=0, concat_axis=0, tiled=True)
    features = heads * across * width
    grad_attn, pay, scale = call(
        functools.partial(own_gradient_state, features),
        [(block, bf16), ((ROW, depth, width), f32), ((tokens, width), f32)],
        product,
        [pltpu.VMEM((8, width), f32)],
    )(decayed, grad_out, attention, sums)

    got = exchange(pay, groups)
    (total,) = call(backward_row, [((depth + META, width), f32)], got.size)(got, facts)
    near = passed_along(total, -ROW)
    normed, query_grad, key_inner, value_inner = call(
        inner_gradients,
        [(block, bf16), (block, bf16), (block, f32), (block, f32)],
        4 * square + product,
    )(
        query_rows,
        key_rows,
        value_rows,
        grad_attn,
        scores,
        state,
        rows,
        cols,
        attention,
        scale,
    )
    near, key_inner, value_inner = lax.optimization_barrier((near, key_inner, value_inner))
    (states,) = call(backward_scan, [((ROW, depth, width), f32)], got.size)(got, facts, near)
    back = exchange(states, groups)
    key_grad, value_grad = call(
        outer_gradients,
        [(block, bf16), (block, bf16)],
        2 * product,
        [
            pltpu.VMEM(block, bf16),
            pltpu.VMEM(block, bf16),
            pltpu.SemaphoreType.DMA((2 * heads,)),
        ],
        to_hbm=True,
    )(key_rows, value_rows, key_inner, value_inner, back, cols)
    return normed, query_grad, key_grad, value_grad


def solution(mesh):
    rows = P("head", "seq", None)
    return jax.shard_map(
        per_device,
        mesh=mesh,
        in_specs=(rows, rows, rows, P("head", "seq"), P("seq"), rows),
        out_specs=(rows, rows, rows, rows),
        check_vma=False,
    )
```

```python
import functools

import jax
import jax.numpy as jnp
from jax import lax
from jax.experimental import pallas as pl
from jax.experimental.pallas import tpu as pltpu
from jax.sharding import PartitionSpec as P

EPSILON = 1e-06
ROW = 16
LEAD = 4
LATER = 4
META = 8
HIGH = lax.Precision.HIGHEST


def dot(a, b, da, db):
    return lax.dot_general(
        a, b, (((da,), (db,)), ((), ())), preferred_element_type=jnp.float32
    )


def later(member):
    return (member + ROW - LATER) % ROW


def listed():
    lead = jnp.where(lax.axis_index("seq") < ROW, 0, LEAD)
    return lambda member: lax.rem(member + ROW - lead, ROW)


def call(body, outs, flops, scratch=(), from_hbm=False, to_hbm=False):
    shapes = [jax.ShapeDtypeStruct(s, d) for s, d in outs]

    def run(*args):
        size = sum(a.size * a.dtype.itemsize for a in (*args, *shapes))
        return pl.pallas_call(
            body,
            out_shape=shapes,
            in_specs=[pl.BlockSpec(memory_space=pltpu.HBM if from_hbm else pltpu.VMEM)] * len(args),
            out_specs=[pl.BlockSpec(memory_space=pltpu.HBM if to_hbm else pltpu.VMEM)] * len(shapes),
            scratch_shapes=list(scratch),
            cost_estimate=pl.CostEstimate(flops=flops, bytes_accessed=size, transcendentals=0),
            compiler_params=pltpu.CompilerParams(vmem_limit_bytes=8 << 20),
            name=body.__name__ if hasattr(body, "__name__") else body.func.__name__,
        )(*args)

    return run


def running_sums(gates, ones):
    high = gates.astype(jnp.bfloat16)
    rest = gates - high.astype(jnp.float32)
    middle = rest.astype(jnp.bfloat16)
    low = (rest - middle.astype(jnp.float32)).astype(jnp.bfloat16)
    return dot(low, ones, 1, 0) + dot(middle, ones, 1, 0) + dot(high, ones, 1, 0)


def local_states(
    gate_hbm, ep_hbm, k_hbm, v_hbm, pay_ref, rows_ref, gate_ref, ep_ref, k_ref, v_ref, sems
):
    heads, tokens = gate_ref.shape
    width = k_ref.shape[2]
    per_head = ROW // heads
    depth = width // per_head
    slot = listed()
    gates = pltpu.make_async_copy(gate_hbm, gate_ref, sems.at[0])
    ids = pltpu.make_async_copy(ep_hbm, ep_ref, sems.at[1])
    gates.start()
    ids.start()
    keys = [pltpu.make_async_copy(k_hbm.at[h], k_ref.at[h], sems.at[2 + h]) for h in range(heads)]
    values = [
        pltpu.make_async_copy(v_hbm.at[h], v_ref.at[h], sems.at[2 + heads + h])
        for h in range(heads)
    ]
    for copy in (*keys, *values):
        copy.start()
    rows_ref[...] = jnp.zeros(rows_ref.shape, jnp.float32)
    upto = lax.broadcasted_iota(jnp.int32, (tokens, tokens), 0)
    place = lax.broadcasted_iota(jnp.int32, (tokens, tokens), 1)
    ones = jnp.where(upto <= place, 1.0, 0.0).astype(jnp.bfloat16)
    gates.wait()
    run = running_sums(gate_ref[...], ones)
    total = run[:, tokens - 1 :]
    ids.wait()
    ep = ep_ref[...]
    first, last = ep[:, :1], ep[:, tokens - 1 :]
    leave = jnp.where(ep == last, jnp.exp(total - run), 0.0)
    rows_ref[0:heads] = run
    rows_ref[heads : 2 * heads] = jnp.where(ep == first, jnp.exp(run), 0.0)
    rows_ref[2 * heads : 3 * heads] = leave
    rows_ref[3 * heads : 3 * heads + 1] = ep.astype(jnp.float32)
    fact = lax.broadcasted_iota(jnp.int32, (1, width), 1)
    first_f, last_f = first.astype(jnp.float32), last.astype(jnp.float32)
    for copy in (*keys, *values):
        copy.wait()
    for h in range(heads):
        decayed = (k_ref[h].T.astype(jnp.float32) * leave[h : h + 1]).astype(jnp.bfloat16)
        state = dot(decayed, v_ref[h], 1, 0)
        facts = jnp.where(
            fact == 0,
            total[h : h + 1],
            jnp.where(fact == 1, first_f, jnp.where(fact == 2, last_f, 0.0)),
        )
        for part in range(per_head):
            at = slot(h * per_head + part) * (depth + 1)
            pay_ref[pl.ds(at, depth)] = state[part * depth : (part + 1) * depth]
            pay_ref[pl.ds(at + depth, 1)] = facts


def facts_of(fact_ref, j):
    return fact_ref[j, 0:1], fact_ref[j, 1:2], fact_ref[j, 2:3]


def summary(sum_ref, state, mark):
    depth = state.shape[0]
    row = lax.broadcasted_iota(jnp.int32, (META, state.shape[1]), 0)
    sum_ref[0:depth] = state
    sum_ref[depth : depth + META] = jnp.where(row == 1, mark, 0.0)


def forward_row(got_ref, sum_ref, fact_ref):
    stride = got_ref.shape[0] // ROW
    depth, shape = stride - 1, (1, got_ref.shape[1])
    slot = listed()
    for j in range(ROW):
        facts = got_ref[pl.ds(slot(j) * stride + depth, 1)]
        for i in range(3):
            fact_ref[j, i : i + 1] = jnp.broadcast_to(facts[:, i : i + 1], shape)
    state, mark = got_ref[pl.ds(slot(0) * stride, depth)], facts_of(fact_ref, 0)[2]
    for j in range(1, ROW):
        decay, _, last = facts_of(fact_ref, j)
        kept = jnp.where(mark == last, jnp.exp(decay), 0.0)
        state = kept * state + got_ref[pl.ds(slot(j) * stride, depth)]
        mark = last
    summary(sum_ref, state, mark)


def backward_row(got_ref, fact_ref, sum_ref):
    state, mark = got_ref[later(ROW - 1)], facts_of(fact_ref, ROW - 1)[1]
    for j in range(ROW - 2, -1, -1):
        decay, first, _ = facts_of(fact_ref, j)
        state = jnp.where(mark == first, jnp.exp(decay), 0.0) * state + got_ref[later(j)]
        mark = first
    summary(sum_ref, state, mark)


def forward_scan(got_ref, fact_ref, near_ref, out_ref):
    depth = out_ref.shape[1]
    slot = listed()
    state, mark = near_ref[0:depth], near_ref[depth + 1 : depth + 2]
    for j in range(ROW):
        decay, first, last = facts_of(fact_ref, j)
        out_ref[later(j)] = jnp.where(mark == first, state, 0.0)
        kept = jnp.where(mark == last, jnp.exp(decay), 0.0)
        state = kept * state + got_ref[pl.ds(slot(j) * (depth + 1), depth)]
        mark = last


def backward_scan(got_ref, fact_ref, near_ref, out_ref):
    depth = out_ref.shape[1]
    state, mark = near_ref[0:depth], near_ref[depth + 1 : depth + 2]
    for j in range(ROW - 1, -1, -1):
        decay, first, last = facts_of(fact_ref, j)
        out_ref[later(j)] = jnp.where(mark == last, state, 0.0)
        state = jnp.where(mark == first, jnp.exp(decay), 0.0) * state + got_ref[later(j)]
        mark = first


def head_state(state_ref, heads, h):
    per_head = ROW // heads
    slices = [state_ref[later(h * per_head + part)] for part in range(per_head)]
    return jnp.concatenate(slices, axis=0).astype(jnp.bfloat16)


def decays_of(rows_ref, cols_ref, heads, h):
    tokens = cols_ref.shape[0]
    later = lax.broadcasted_iota(jnp.int32, (tokens, tokens), 0)
    earlier = lax.broadcasted_iota(jnp.int32, (tokens, tokens), 1)
    one = 3 * heads
    allowed = (cols_ref[:, one : one + 1] == rows_ref[one : one + 1]) & (later >= earlier)
    difference = cols_ref[:, h : h + 1] - rows_ref[h : h + 1]
    return jnp.where(allowed, jnp.exp(jnp.where(allowed, difference, 0.0)), 0.0)


def within_stretch(
    q_ref, k_ref, v_ref, rows_ref, scores_ref, within_ref, decayed_ref, cols_ref
):
    heads = q_ref.shape[0]
    cols_ref[...] = rows_ref[...].T
    for h in range(heads):
        decays = decays_of(rows_ref, cols_ref, heads, h)
        scores = (dot(q_ref[h], k_ref[h], 1, 1) * decays).astype(jnp.bfloat16)
        scores_ref[h] = scores
        within_ref[h] = dot(scores, v_ref[h], 1, 0)
        enter = rows_ref[heads + h : heads + h + 1]
        decayed_ref[h] = (q_ref[h].astype(jnp.float32).T * enter).astype(jnp.bfloat16)


def attend(q_ref, g_ref, state_ref, within_ref, cols_ref, att_ref, sums_ref):
    heads, tokens, width = q_ref.shape
    squares = crossed = jnp.zeros((tokens, width), jnp.float32)
    for h in range(heads):
        state = head_state(state_ref, heads, h)
        enter = cols_ref[:, heads + h : heads + h + 1]
        att = within_ref[h] + dot(q_ref[h], state, 1, 0) * enter
        att_ref[h] = att
        squares = squares + att * att
        crossed = crossed + g_ref[h].astype(jnp.float32) * att
    at = 0
    for terms in (squares, crossed):
        line = jnp.sum(terms.T, axis=0, keepdims=True)
        for start in range(0, tokens, width):
            piece = line[:, start : start + width]
            for p in range(sums_ref.shape[0]):
                sums_ref[p, at : at + 1] = piece
            at += 1


def own_gradient_state(
    features, decayed_ref, g_ref, att_ref, sums_ref, ga_ref, pay_ref, scale_ref, tmp_ref
):
    heads, _, width = g_ref.shape
    per_head = ROW // heads
    depth = width // per_head
    half = sums_ref.shape[1] // 2
    sums = jnp.sum(sums_ref[...], axis=0)
    root = jnp.sqrt(sums[:half] / features + EPSILON)
    tmp_ref[0:half] = 1.0 / root
    tmp_ref[half : 2 * half] = sums[half:] / (features * root * root)
    upright = tmp_ref[...].T
    shape = scale_ref.shape
    inverse = jnp.concatenate([upright[:, i : i + 1] for i in range(half)], axis=0)
    factor = jnp.concatenate([upright[:, i : i + 1] for i in range(half, 2 * half)], axis=0)
    inverse, factor = jnp.broadcast_to(inverse, shape), jnp.broadcast_to(factor, shape)
    scale_ref[...] = inverse
    for h in range(heads):
        ga = ((g_ref[h].astype(jnp.float32) - att_ref[h] * factor) * inverse).astype(jnp.bfloat16)
        ga_ref[h] = ga
        back = dot(decayed_ref[h], ga, 1, 0)
        for part in range(per_head):
            pay_ref[later(h * per_head + part)] = back[part * depth : (part + 1) * depth]


def inner_gradients(
    q_ref,
    k_ref,
    v_ref,
    ga_ref,
    scores_ref,
    state_ref,
    rows_ref,
    cols_ref,
    att_ref,
    scale_ref,
    norm_ref,
    gq_ref,
    ki_ref,
    vi_ref,
):
    heads = q_ref.shape[0]
    for h in range(heads):
        norm_ref[h] = (att_ref[h] * scale_ref[...]).astype(jnp.bfloat16)
        ga = ga_ref[h]
        decays = decays_of(rows_ref, cols_ref, heads, h)
        slope = (dot(ga, v_ref[h], 1, 1) * decays).astype(jnp.bfloat16)
        enter = cols_ref[:, heads + h : heads + h + 1]
        state = head_state(state_ref, heads, h)
        gq_ref[h] = (dot(slope, k_ref[h], 1, 0) + dot(ga, state, 1, 1) * enter).astype(jnp.bfloat16)
        ki_ref[h] = dot(slope, q_ref[h], 0, 0)
        vi_ref[h] = dot(scores_ref[h], ga, 0, 0)


def outer_gradients(
    k_ref, v_ref, ki_ref, vi_ref, back_ref, cols_ref, gk_hbm, gv_hbm, gk_ref, gv_ref, sems
):
    heads = k_ref.shape[0]
    copies = []
    for h in range(heads):
        back = head_state(back_ref, heads, h)
        leave = cols_ref[:, 2 * heads + h : 2 * heads + h + 1]
        gk_ref[h] = (ki_ref[h] + dot(v_ref[h], back, 1, 1) * leave).astype(jnp.bfloat16)
        copies.append(pltpu.make_async_copy(gk_ref.at[h], gk_hbm.at[h], sems.at[2 * h]))
        copies[-1].start()
        gv_ref[h] = (vi_ref[h] + dot(k_ref[h], back, 1, 0) * leave).astype(jnp.bfloat16)
        copies.append(pltpu.make_async_copy(gv_ref.at[h], gv_hbm.at[h], sems.at[2 * h + 1]))
        copies[-1].start()
    for copy in copies:
        copy.wait()


def in_hbm(array):
    return pltpu.with_memory_space_constraint(array, pltpu.HBM)


def exchange(block, groups):
    return lax.all_to_all(
        block, "seq", split_axis=0, concat_axis=0, tiled=True, axis_index_groups=groups
    )


def passed_along(block, distance):
    devices = range(lax.axis_size("seq"))
    route = [(i, i + distance) for i in devices if i + distance in devices]
    return lax.ppermute(block, "seq", route)


def per_device(query_rows, key_rows, value_rows, log_gate, episode, grad_out):
    heads, tokens, width = query_rows.shape
    depth = heads * width // ROW
    devices = lax.axis_size("seq")
    starts = range(0, devices, ROW)
    first = [[at + (i + (LEAD if at else 0)) % ROW for i in range(ROW)] for at in starts]
    groups = [[at + (i + LATER) % ROW for i in range(ROW)] for at in starts]
    f32, bf16 = jnp.float32, jnp.bfloat16
    block = (heads, tokens, width)
    product = 2 * heads * tokens * width * width
    square = 2 * heads * tokens * tokens * width
    line = 128

    pay, rows = call(
        local_states,
        [
            ((ROW * (depth + 1), width), f32),
            ((line, tokens), f32),
        ],
        product,
        [
            pltpu.VMEM((heads, tokens), f32),
            pltpu.VMEM((1, tokens), jnp.int32),
            pltpu.VMEM(block, bf16),
            pltpu.VMEM(block, bf16),
            pltpu.SemaphoreType.DMA((2 + 2 * heads,)),
        ],
        from_hbm=True,
    )(*map(in_hbm, (log_gate, episode.reshape(1, tokens), key_rows, value_rows)))
    dense = (ROW, depth + 1, 1, width)
    got = exchange(pay.reshape(dense), first).reshape(pay.shape)
    total, facts = call(
        forward_row, [((depth + META, width), f32), ((ROW, META, width), f32)], got.size
    )(got)
    near = passed_along(total, ROW)
    scores, within, decayed, cols = call(
        within_stretch,
        [
            ((heads, tokens, tokens), bf16),
            (block, f32),
            ((heads, width, tokens), bf16),
            ((tokens, line), f32),
        ],
        2 * square,
    )(query_rows, key_rows, value_rows, rows)
    near, within = lax.optimization_barrier((near, within))
    (states,) = call(forward_scan, [((ROW, depth, width), f32)], got.size)(got, facts, near)
    state = exchange(states, groups)

    lines = 2 * tokens // width
    across = lax.axis_size("head")
    attention, sums = call(attend, [(block, f32), ((across, lines, width), f32)], product)(
        query_rows, grad_out, state, within, cols
    )
    order = [[(i + across - 2) % across for i in range(across)]]
    sums = lax.all_to_all(
        sums, "head", split_axis=0, concat_axis=0, tiled=True, axis_index_groups=order
    )
    features = heads * across * width
    grad_attn, pay, scale = call(
        functools.partial(own_gradient_state, features),
        [(block, bf16), ((ROW, depth, width), f32), ((tokens, width), f32)],
        product,
        [pltpu.VMEM((8, width), f32)],
    )(decayed, grad_out, attention, sums)

    got = exchange(pay, groups)
    (total,) = call(backward_row, [((depth + META, width), f32)], got.size)(got, facts)
    near = passed_along(total, -ROW)
    normed, query_grad, key_inner, value_inner = call(
        inner_gradients,
        [(block, bf16), (block, bf16), (block, f32), (block, f32)],
        4 * square + product,
    )(
        query_rows,
        key_rows,
        value_rows,
        grad_attn,
        scores,
        state,
        rows,
        cols,
        attention,
        scale,
    )
    near, key_inner, value_inner = lax.optimization_barrier((near, key_inner, value_inner))
    (states,) = call(backward_scan, [((ROW, depth, width), f32)], got.size)(got, facts, near)
    back = exchange(states, groups)
    key_grad, value_grad = call(
        outer_gradients,
        [(block, bf16), (block, bf16)],
        2 * product,
        [
            pltpu.VMEM(block, bf16),
            pltpu.VMEM(block, bf16),
            pltpu.SemaphoreType.DMA((2 * heads,)),
        ],
        to_hbm=True,
    )(key_rows, value_rows, key_inner, value_inner, back, cols)
    return normed, query_grad, key_grad, value_grad


def solution(mesh):
    rows = P("head", "seq", None)
    return jax.shard_map(
        per_device,
        mesh=mesh,
        in_specs=(rows, rows, rows, P("head", "seq"), P("seq"), rows),
        out_specs=(rows, rows, rows, rows),
        check_vma=False,
    )
```

```python
import functools

import jax
import jax.numpy as jnp
from jax import lax
from jax.experimental import pallas as pl
from jax.experimental.pallas import tpu as pltpu
from jax.sharding import PartitionSpec as P

EPSILON = 1e-06
ROW = 16
LEAD = 4
LATER = 4
META = 8
HIGH = lax.Precision.HIGHEST


def dot(a, b, da, db):
    return lax.dot_general(
        a, b, (((da,), (db,)), ((), ())), preferred_element_type=jnp.float32
    )


def later(member):
    return (member + ROW - LATER) % ROW


def listed():
    lead = jnp.where(lax.axis_index("seq") < ROW, 0, LEAD)
    return lambda member: lax.rem(member + ROW - lead, ROW)


def call(body, outs, flops, scratch=(), from_hbm=False, to_hbm=False):
    shapes = [jax.ShapeDtypeStruct(s, d) for s, d in outs]

    def run(*args):
        size = sum(a.size * a.dtype.itemsize for a in (*args, *shapes))
        return pl.pallas_call(
            body,
            out_shape=shapes,
            in_specs=[pl.BlockSpec(memory_space=pltpu.HBM if from_hbm else pltpu.VMEM)] * len(args),
            out_specs=[pl.BlockSpec(memory_space=pltpu.HBM if to_hbm else pltpu.VMEM)] * len(shapes),
            scratch_shapes=list(scratch),
            cost_estimate=pl.CostEstimate(flops=flops, bytes_accessed=size, transcendentals=0),
            compiler_params=pltpu.CompilerParams(vmem_limit_bytes=8 << 20),
            name=body.__name__ if hasattr(body, "__name__") else body.func.__name__,
        )(*args)

    return run


def running_sums(gates, ones):
    high = gates.astype(jnp.bfloat16)
    rest = gates - high.astype(jnp.float32)
    middle = rest.astype(jnp.bfloat16)
    low = (rest - middle.astype(jnp.float32)).astype(jnp.bfloat16)
    return dot(low, ones, 1, 0) + dot(middle, ones, 1, 0) + dot(high, ones, 1, 0)


def local_states(
    gate_hbm, ep_hbm, k_hbm, v_hbm, pay_ref, rows_ref, gate_ref, ep_ref, k_ref, v_ref, sems
):
    heads, tokens = gate_ref.shape
    width = k_ref.shape[2]
    per_head = ROW // heads
    depth = width // per_head
    slot = listed()
    gates = pltpu.make_async_copy(gate_hbm, gate_ref, sems.at[0])
    ids = pltpu.make_async_copy(ep_hbm, ep_ref, sems.at[1])
    gates.start()
    ids.start()
    keys = [pltpu.make_async_copy(k_hbm.at[h], k_ref.at[h], sems.at[2 + h]) for h in range(heads)]
    values = [
        pltpu.make_async_copy(v_hbm.at[h], v_ref.at[h], sems.at[2 + heads + h])
        for h in range(heads)
    ]
    for copy in (*keys, *values):
        copy.start()
    rows_ref[...] = jnp.zeros(rows_ref.shape, jnp.float32)
    upto = lax.broadcasted_iota(jnp.int32, (tokens, tokens), 0)
    place = lax.broadcasted_iota(jnp.int32, (tokens, tokens), 1)
    ones = jnp.where(upto <= place, 1.0, 0.0).astype(jnp.bfloat16)
    gates.wait()
    run = running_sums(gate_ref[...], ones)
    total = run[:, tokens - 1 :]
    ids.wait()
    ep = ep_ref[...]
    first, last = ep[:, :1], ep[:, tokens - 1 :]
    leave = jnp.where(ep == last, jnp.exp(total - run), 0.0)
    rows_ref[0:heads] = run
    rows_ref[heads : 2 * heads] = jnp.where(ep == first, jnp.exp(run), 0.0)
    rows_ref[2 * heads : 3 * heads] = leave
    rows_ref[3 * heads : 3 * heads + 1] = ep.astype(jnp.float32)
    fact = lax.broadcasted_iota(jnp.int32, (1, width), 1)
    first_f, last_f = first.astype(jnp.float32), last.astype(jnp.float32)
    for copy in (*keys, *values):
        copy.wait()
    for h in range(heads):
        decayed = (k_ref[h].T.astype(jnp.float32) * leave[h : h + 1]).astype(jnp.bfloat16)
        state = dot(decayed, v_ref[h], 1, 0)
        facts = jnp.where(
            fact == 0,
            total[h : h + 1],
            jnp.where(fact == 1, first_f, jnp.where(fact == 2, last_f, 0.0)),
        )
        for part in range(per_head):
            at = slot(h * per_head + part) * (depth + 1)
            pay_ref[pl.ds(at, depth)] = state[part * depth : (part + 1) * depth]
            pay_ref[pl.ds(at + depth, 1)] = facts


def facts_of(fact_ref, j):
    return fact_ref[j, 0:1], fact_ref[j, 1:2], fact_ref[j, 2:3]


def summary(sum_ref, state, mark):
    depth = state.shape[0]
    row = lax.broadcasted_iota(jnp.int32, (META, state.shape[1]), 0)
    sum_ref[0:depth] = state
    sum_ref[depth : depth + META] = jnp.where(row == 1, mark, 0.0)


def forward_row(got_ref, sum_ref, fact_ref):
    stride = got_ref.shape[0] // ROW
    depth, shape = stride - 1, (1, got_ref.shape[1])
    slot = listed()
    for j in range(ROW):
        facts = got_ref[pl.ds(slot(j) * stride + depth, 1)]
        for i in range(3):
            fact_ref[j, i : i + 1] = jnp.broadcast_to(facts[:, i : i + 1], shape)
    state, mark = got_ref[pl.ds(slot(0) * stride, depth)], facts_of(fact_ref, 0)[2]
    for j in range(1, ROW):
        decay, _, last = facts_of(fact_ref, j)
        kept = jnp.where(mark == last, jnp.exp(decay), 0.0)
        state = kept * state + got_ref[pl.ds(slot(j) * stride, depth)]
        mark = last
    summary(sum_ref, state, mark)


def backward_row(got_ref, fact_ref, sum_ref):
    state, mark = got_ref[later(ROW - 1)], facts_of(fact_ref, ROW - 1)[1]
    for j in range(ROW - 2, -1, -1):
        decay, first, _ = facts_of(fact_ref, j)
        state = jnp.where(mark == first, jnp.exp(decay), 0.0) * state + got_ref[later(j)]
        mark = first
    summary(sum_ref, state, mark)


def forward_scan(got_ref, fact_ref, near_ref, out_ref):
    depth = out_ref.shape[1]
    slot = listed()
    state, mark = near_ref[0:depth], near_ref[depth + 1 : depth + 2]
    for j in range(ROW):
        decay, first, last = facts_of(fact_ref, j)
        out_ref[later(j)] = jnp.where(mark == first, state, 0.0)
        kept = jnp.where(mark == last, jnp.exp(decay), 0.0)
        state = kept * state + got_ref[pl.ds(slot(j) * (depth + 1), depth)]
        mark = last


def backward_scan(got_ref, fact_ref, near_ref, out_ref):
    depth = out_ref.shape[1]
    state, mark = near_ref[0:depth], near_ref[depth + 1 : depth + 2]
    for j in range(ROW - 1, -1, -1):
        decay, first, last = facts_of(fact_ref, j)
        out_ref[later(j)] = jnp.where(mark == last, state, 0.0)
        state = jnp.where(mark == first, jnp.exp(decay), 0.0) * state + got_ref[later(j)]
        mark = first


def head_state(state_ref, heads, h):
    per_head = ROW // heads
    slices = [state_ref[later(h * per_head + part)] for part in range(per_head)]
    return jnp.concatenate(slices, axis=0).astype(jnp.bfloat16)


def decays_of(rows_ref, cols_ref, heads, h):
    tokens = cols_ref.shape[0]
    later = lax.broadcasted_iota(jnp.int32, (tokens, tokens), 0)
    earlier = lax.broadcasted_iota(jnp.int32, (tokens, tokens), 1)
    one = 3 * heads
    allowed = (cols_ref[:, one : one + 1] == rows_ref[one : one + 1]) & (later >= earlier)
    difference = cols_ref[:, h : h + 1] - rows_ref[h : h + 1]
    return jnp.where(allowed, jnp.exp(jnp.where(allowed, difference, 0.0)), 0.0)


def within_stretch(
    q_ref, k_ref, v_ref, rows_ref, scores_ref, within_ref, decayed_ref, cols_ref
):
    heads = q_ref.shape[0]
    cols_ref[...] = rows_ref[...].T
    for h in range(heads):
        decays = decays_of(rows_ref, cols_ref, heads, h)
        scores = (dot(q_ref[h], k_ref[h], 1, 1) * decays).astype(jnp.bfloat16)
        scores_ref[h] = scores
        within_ref[h] = dot(scores, v_ref[h], 1, 0)
        enter = rows_ref[heads + h : heads + h + 1]
        decayed_ref[h] = (q_ref[h].astype(jnp.float32).T * enter).astype(jnp.bfloat16)


def attend(q_ref, g_ref, state_ref, within_ref, cols_ref, att_ref, sums_ref):
    heads, tokens, width = q_ref.shape
    squares = crossed = jnp.zeros((tokens, width), jnp.float32)
    for h in range(heads):
        state = head_state(state_ref, heads, h)
        enter = cols_ref[:, heads + h : heads + h + 1]
        att = within_ref[h] + dot(q_ref[h], state, 1, 0) * enter
        att_ref[h] = att
        squares = squares + att * att
        crossed = crossed + g_ref[h].astype(jnp.float32) * att
    at = 0
    for terms in (squares, crossed):
        line = jnp.sum(terms.T, axis=0, keepdims=True)
        for start in range(0, tokens, width):
            piece = line[:, start : start + width]
            for p in range(sums_ref.shape[0]):
                sums_ref[p, at : at + 1] = piece
            at += 1


def own_gradient_state(
    features, decayed_ref, g_ref, att_ref, sums_ref, ga_ref, pay_ref, scale_ref, tmp_ref
):
    heads, _, width = g_ref.shape
    per_head = ROW // heads
    depth = width // per_head
    half = sums_ref.shape[1] // 2
    sums = jnp.sum(sums_ref[...], axis=0)
    root = jnp.sqrt(sums[:half] / features + EPSILON)
    tmp_ref[0:half] = 1.0 / root
    tmp_ref[half : 2 * half] = sums[half:] / (features * root * root)
    upright = tmp_ref[...].T
    shape = scale_ref.shape
    inverse = jnp.concatenate([upright[:, i : i + 1] for i in range(half)], axis=0)
    factor = jnp.concatenate([upright[:, i : i + 1] for i in range(half, 2 * half)], axis=0)
    inverse, factor = jnp.broadcast_to(inverse, shape), jnp.broadcast_to(factor, shape)
    scale_ref[...] = inverse
    for h in range(heads):
        ga = ((g_ref[h].astype(jnp.float32) - att_ref[h] * factor) * inverse).astype(jnp.bfloat16)
        ga_ref[h] = ga
        back = dot(decayed_ref[h], ga, 1, 0)
        for part in range(per_head):
            pay_ref[later(h * per_head + part)] = back[part * depth : (part + 1) * depth]


def inner_gradients(
    q_ref,
    k_ref,
    v_ref,
    ga_ref,
    scores_ref,
    state_ref,
    rows_ref,
    cols_ref,
    att_ref,
    scale_ref,
    norm_ref,
    gq_ref,
    ki_ref,
    vi_ref,
):
    heads = q_ref.shape[0]
    for h in range(heads):
        norm_ref[h] = (att_ref[h] * scale_ref[...]).astype(jnp.bfloat16)
        ga = ga_ref[h]
        decays = decays_of(rows_ref, cols_ref, heads, h)
        slope = (dot(ga, v_ref[h], 1, 1) * decays).astype(jnp.bfloat16)
        enter = cols_ref[:, heads + h : heads + h + 1]
        state = head_state(state_ref, heads, h)
        gq_ref[h] = (dot(slope, k_ref[h], 1, 0) + dot(ga, state, 1, 1) * enter).astype(jnp.bfloat16)
        ki_ref[h] = dot(slope, q_ref[h], 0, 0)
        vi_ref[h] = dot(scores_ref[h], ga, 0, 0)


def outer_gradients(
    k_ref, v_ref, ki_ref, vi_ref, back_ref, cols_ref, gk_hbm, gv_hbm, gk_ref, gv_ref, sems
):
    heads = k_ref.shape[0]
    copies = []
    for h in range(heads):
        back = head_state(back_ref, heads, h)
        leave = cols_ref[:, 2 * heads + h : 2 * heads + h + 1]
        gk_ref[h] = (ki_ref[h] + dot(v_ref[h], back, 1, 1) * leave).astype(jnp.bfloat16)
        copies.append(pltpu.make_async_copy(gk_ref.at[h], gk_hbm.at[h], sems.at[2 * h]))
        copies[-1].start()
        gv_ref[h] = (vi_ref[h] + dot(k_ref[h], back, 1, 0) * leave).astype(jnp.bfloat16)
        copies.append(pltpu.make_async_copy(gv_ref.at[h], gv_hbm.at[h], sems.at[2 * h + 1]))
        copies[-1].start()
    for copy in copies:
        copy.wait()


def in_hbm(array):
    return pltpu.with_memory_space_constraint(array, pltpu.HBM)


def exchange(block, groups):
    return lax.all_to_all(
        block, "seq", split_axis=0, concat_axis=0, tiled=True, axis_index_groups=groups
    )


def passed_along(block, distance):
    devices = range(lax.axis_size("seq"))
    route = [(i, i + distance) for i in devices if i + distance in devices]
    return lax.ppermute(block, "seq", route)


def per_device(query_rows, key_rows, value_rows, log_gate, episode, grad_out):
    heads, tokens, width = query_rows.shape
    depth = heads * width // ROW
    devices = lax.axis_size("seq")
    starts = range(0, devices, ROW)
    first = [[at + (i + (LEAD if at else 0)) % ROW for i in range(ROW)] for at in starts]
    groups = [[at + (i + LATER) % ROW for i in range(ROW)] for at in starts]
    f32, bf16 = jnp.float32, jnp.bfloat16
    block = (heads, tokens, width)
    product = 2 * heads * tokens * width * width
    square = 2 * heads * tokens * tokens * width
    line = 128

    pay, rows = call(
        local_states,
        [
            ((ROW * (depth + 1), width), f32),
            ((line, tokens), f32),
        ],
        product,
        [
            pltpu.VMEM((heads, tokens), f32),
            pltpu.VMEM((1, tokens), jnp.int32),
            pltpu.VMEM(block, bf16),
            pltpu.VMEM(block, bf16),
            pltpu.SemaphoreType.DMA((2 + 2 * heads,)),
        ],
        from_hbm=True,
    )(*map(in_hbm, (log_gate, episode.reshape(1, tokens), key_rows, value_rows)))
    dense = (ROW, depth + 1, 1, width)
    got = exchange(pay.reshape(dense), first).reshape(pay.shape)
    total, facts = call(
        forward_row, [((depth + META, width), f32), ((ROW, META, width), f32)], got.size
    )(got)
    near = passed_along(total, ROW)
    scores, within, decayed, cols = call(
        within_stretch,
        [
            ((heads, tokens, tokens), bf16),
            (block, f32),
            ((heads, width, tokens), bf16),
            ((tokens, line), f32),
        ],
        2 * square,
    )(query_rows, key_rows, value_rows, rows)
    near, within = lax.optimization_barrier((near, within))
    (states,) = call(forward_scan, [((ROW, depth, width), f32)], got.size)(got, facts, near)
    state = exchange(states, groups)

    lines = 2 * tokens // width
    across = lax.axis_size("head")
    attention, sums = call(attend, [(block, f32), ((across, lines, width), f32)], product)(
        query_rows, grad_out, state, within, cols
    )
    order = [[(i + across - 4) % across for i in range(across)]]
    sums = lax.all_to_all(
        sums, "head", split_axis=0, concat_axis=0, tiled=True, axis_index_groups=order
    )
    features = heads * across * width
    grad_attn, pay, scale = call(
        functools.partial(own_gradient_state, features),
        [(block, bf16), ((ROW, depth, width), f32), ((tokens, width), f32)],
        product,
        [pltpu.VMEM((8, width), f32)],
    )(decayed, grad_out, attention, sums)

    got = exchange(pay, groups)
    (total,) = call(backward_row, [((depth + META, width), f32)], got.size)(got, facts)
    near = passed_along(total, -ROW)
    normed, query_grad, key_inner, value_inner = call(
        inner_gradients,
        [(block, bf16), (block, bf16), (block, f32), (block, f32)],
        4 * square + product,
    )(
        query_rows,
        key_rows,
        value_rows,
        grad_attn,
        scores,
        state,
        rows,
        cols,
        attention,
        scale,
    )
    near, key_inner, value_inner = lax.optimization_barrier((near, key_inner, value_inner))
    (states,) = call(backward_scan, [((ROW, depth, width), f32)], got.size)(got, facts, near)
    back = exchange(states, groups)
    key_grad, value_grad = call(
        outer_gradients,
        [(block, bf16), (block, bf16)],
        2 * product,
        [
            pltpu.VMEM(block, bf16),
            pltpu.VMEM(block, bf16),
            pltpu.SemaphoreType.DMA((2 * heads,)),
        ],
        to_hbm=True,
    )(key_rows, value_rows, key_inner, value_inner, back, cols)
    return normed, query_grad, key_grad, value_grad


def solution(mesh):
    rows = P("head", "seq", None)
    return jax.shard_map(
        per_device,
        mesh=mesh,
        in_specs=(rows, rows, rows, P("head", "seq"), P("seq"), rows),
        out_specs=(rows, rows, rows, rows),
        check_vma=False,
    )
```
